256 devices in a mesh: inner: 16 (over x, y), outer: 16 (over z, core).
Axes of the slice: x: 4, y: 4, z: 8, core: 2. Of those that a mesh axis runs over, the one named last changes fastest.
Arguments:
- tokens: int32 [4096], P('outer'), may hold values from 0 to 16383
- step_index: int32 [1], replicated, may hold values from 0 to 31
- embed_table: bfloat16 [16384, 2048], P(None, 'inner'), may hold values from -6 to 6
- gain_one: float32 [2048], replicated, may hold values from 0.5 to 1.5
- gate_weight: bfloat16 [2048, 5632], P(None, 'inner'), may hold values from -0.125 to 0.125
- up_weight: bfloat16 [2048, 5632], P(None, 'inner'), may hold values from -0.125 to 0.125
- down_weight: bfloat16 [5632, 2048], P('inner'), may hold values from -0.078125 to 0.078125
- gain_two: float32 [2048], replicated, may hold values from 0.5 to 1.5
- query_weight: bfloat16 [2048, 2048], P(None, 'inner'), may hold values from -0.125 to 0.125
- key_weight: bfloat16 [2048, 2048], P(None, 'inner'), may hold values from -0.125 to 0.125
- value_weight: bfloat16 [2048, 4096], P(None, 'inner'), may hold values from -0.125 to 0.125
- decay_weight: bfloat16 [2048, 16], P(None, 'inner'), may hold values from -0.125 to 0.125
- beta_weight: bfloat16 [2048, 16], P(None, 'inner'), may hold values from -0.125 to 0.125
- rate_log: float32 [16], P('inner'), may hold values from -12 to -2
- decay_bias: float32 [16], P('inner'), may hold values from -1 to 1
- beta_bias: float32 [16], P('inner'), may hold values from -6 to -2
- cotangent: bfloat16 [4096, 4096], P('outer', 'inner'), may hold values from -192 to 192
Outputs:
- attribution: float32 [4096, 5632], P('outer', 'inner')
The draws below stay inside these ranges and needn't reach their ends.
All inputs are finite; a program needn't handle non-finite values.
Results may differ from the reference program's by a relative error of at most 0.029.
Values may be sent and summed in bfloat16 or wider, within the bound.
A program may use at most 128 MiB of HBM per device.

```python
import functools
import math
import jax
import jax.numpy as jnp
import numpy as np
from jax import lax

D = 2048
FF = 5632
H = 16
KD = 128
VD = 256
VOCAB = 16384
STEPS = 32
TOKENS = 4096
N_INNER = 16


def with_ends(values, stream_key, smallest, top_value):
    shape = values.shape
    spot = [jax.random.randint(jax.random.fold_in(stream_key, axis), (), 0, shape[axis]) for axis in range(len(shape))]
    values = values.at[tuple(spot)].set(smallest)
    longest = shape.index(max(shape))
    spot[longest] = (spot[longest] + 1) % shape[longest]
    return values.at[tuple(spot)].set(top_value)


def steps_of(key, dims, shards, smallest, largest):
    level, own = 1.0, jax.random.fold_in(key, 6)
    for position, parts in shards:
        heights = jnp.exp(jax.random.uniform(jax.random.fold_in(own, position), (parts,), jnp.float32, smallest / len(shards), largest / len(shards)))
        level = level * jnp.repeat(heights, dims[position] // parts).reshape([-1 if axis == position else 1 for axis in range(len(dims))])
    return level


def rank_bounds(count, lean):
    loads = [(1 << 20) // math.isqrt(grade ** lean) + 1 for grade in range(1, count + 1)]
    scale = 1 + sum(loads) // (1 << 30)
    return np.cumsum(np.array([max(1, weight // scale) for weight in loads]))


def skewed_ids(key, shape, number_of, skew):
    grid = rank_bounds(number_of, skew)
    lot = jax.random.randint(jax.random.fold_in(key, 1), shape, 0, int(grid[number_of - 1]))
    grade = jnp.searchsorted(jnp.asarray(grid, jnp.int32), lot, side="right")
    return jax.random.permutation(jax.random.fold_in(key, 2), number_of)[grade].astype(jnp.int32)


def noise(rng, extent, deviation, reach, cuts=(), kind=jnp.bfloat16):
    entries = jax.random.normal(rng, extent, jnp.float32) * deviation
    if len(cuts) > 0:
        entries = steps_of(rng, extent, cuts, -0.22, 0.18) * entries
    return jnp.clip(entries, min=-reach, max=reach).astype(kind)


def setup_inputs(seed: int = 0) -> dict:
    arg_keys = jax.random.split(jax.random.key(seed), 18)
    return {
        "tokens": with_ends(skewed_ids(arg_keys[0], (TOKENS,), VOCAB, 2), jax.random.fold_in(arg_keys[0], 3), 0, VOCAB - 1).astype(jnp.int32),
        "step_index": jax.random.randint(arg_keys[1], (1,), 0, STEPS).astype(jnp.int32),
        "embed_table": noise(arg_keys[2], (VOCAB, D), 1.0, 6.0, ((1, 16),)),
        "gain_one": jnp.clip(1.0 + 0.1 * jax.random.normal(arg_keys[3], (D,), jnp.float32), 0.5, 1.5),
        "gate_weight": noise(arg_keys[4], (D, FF), D ** -0.5, 0.125, ((1, 16),)),
        "up_weight": noise(arg_keys[5], (D, FF), D ** -0.5, 0.125, ((1, 16),)),
        "down_weight": noise(arg_keys[6], (FF, D), FF ** -0.5, 0.078125, ((0, 16),)),
        "gain_two": jnp.clip(1.0 + 0.1 * jax.random.normal(arg_keys[7], (D,), jnp.float32), 0.5, 1.5),
        "query_weight": noise(arg_keys[8], (D, H * KD), D ** -0.5, 0.125, ((1, 16),)),
        "key_weight": noise(arg_keys[9], (D, H * KD), D ** -0.5, 0.125, ((1, 16),)),
        "value_weight": noise(arg_keys[10], (D, H * VD), D ** -0.5, 0.125, ((1, 16),)),
        "decay_weight": noise(arg_keys[11], (D, H), D ** -0.5, 0.125, ((1, 16),)),
        "beta_weight": noise(arg_keys[12], (D, H), D ** -0.5, 0.125, ((1, 16),)),
        "rate_log": jnp.clip(-12.0 + 10.0 * jax.random.uniform(arg_keys[13], (H,), jnp.float32) ** steps_of(arg_keys[13], (H,), ((0, 16),), -0.2, 0.2), -12.0, -2.0),
        "decay_bias": jnp.clip(jax.random.uniform(arg_keys[14], (H,), jnp.float32, -1.0, 1.0) * steps_of(arg_keys[14], (H,), ((0, 16),), -0.4, 0.0), -1.0, 1.0),
        "beta_bias": jnp.clip(-6.0 + 4.0 * jax.random.uniform(arg_keys[15], (H,), jnp.float32) ** steps_of(arg_keys[15], (H,), ((0, 16),), -0.2, 0.2), -6.0, -2.0),
        "cotangent": noise(arg_keys[16], (TOKENS, H * VD), 32.0, 192.0, ((0, 16), (1, 16))),
    }


def unit_rows(values):
    return values * lax.rsqrt(lax.optimization_barrier(jnp.sum(values * values, axis=-1, keepdims=True)) + 1e-06)

def head_inputs(query_rows, key_rows, decay_rows, beta_rows, log_rate, rate_shift, beta_shift):
    queries = unit_rows(query_rows) * query_rows.shape[-1] ** (-0.5)
    keys_unit = unit_rows(key_rows)
    log_decay = -jnp.exp(log_rate) * jax.nn.softplus(decay_rows + rate_shift)
    betas = jax.nn.sigmoid(beta_rows + beta_shift)
    return (queries, keys_unit, log_decay, betas)

def block_step(with_out, state, pieces):
    queries, keys_unit, values, log_decay, betas = pieces
    block_len = keys_unit.shape[0]
    highest = lax.Precision.HIGHEST
    cum_decay = jnp.cumsum(log_decay)
    row_ids = jnp.arange(block_len)[:, None]
    col_ids = jnp.arange(block_len)[None, :]
    lower_mask = row_ids >= col_ids
    decay_mat = jnp.where(lower_mask, jnp.exp(jnp.where(lower_mask, cum_decay[:, None] - cum_decay[None, :], 0.0)), 0.0)
    key_gram = jnp.dot(keys_unit, keys_unit.T, precision=highest)
    strict = jnp.where(row_ids > col_ids, betas[:, None] * decay_mat * key_gram, 0.0)
    system = strict + jnp.eye(block_len, dtype=jnp.float32)
    start_scale = jnp.exp(cum_decay)[:, None]
    target = betas[:, None] * (values - start_scale * jnp.dot(keys_unit, state, precision=highest))
    fresh_vals = lax.linalg.triangular_solve(system, target, left_side=True, lower=True, unit_diagonal=True)
    tail_keys = jnp.exp(cum_decay[-1] - cum_decay)[:, None] * keys_unit
    new_state = jnp.exp(cum_decay[-1]) * state + jnp.dot(tail_keys.T, fresh_vals, precision=highest)
    if with_out:
        scores = decay_mat * jnp.dot(queries, keys_unit.T, precision=highest)
        output = start_scale * jnp.dot(queries, state, precision=highest) + jnp.dot(scores, fresh_vals, precision=highest)
        return (new_state, output)
    return (new_state, None)

def run_blocks(queries, keys_unit, values, log_decay, betas, state, with_out):
    length = keys_unit.shape[0]
    block_len = math.gcd(64, length)
    block_count = length // block_len

    def blocked(array):
        return array.reshape((block_count, block_len) + array.shape[1:])
    step_fn = functools.partial(block_step, with_out)
    final_state, outputs = lax.scan(step_fn, state, (blocked(queries), blocked(keys_unit), blocked(values), blocked(log_decay), blocked(betas)))
    if with_out:
        outputs = outputs.reshape((length,) + outputs.shape[2:])
    return (final_state, outputs)

def rms_scaled(values, gain):
    return values * lax.rsqrt(lax.optimization_barrier(jnp.mean(values * values, axis=-1, keepdims=True)) + 1e-06) * gain

def to_wire(values):
    return lax.optimization_barrier(values.astype(jnp.bfloat16)).astype(jnp.float32)

def head_grads(items):
    query_rows, key_rows, value_rows, decay_rows, beta_rows, cot_rows, log_rate, rate_shift, beta_shift = items

    def target_of(query_in, key_in, value_in, decay_in, beta_in):
        queries, keys_unit, log_decay, betas = head_inputs(query_in, key_in, decay_in, beta_in, log_rate, rate_shift, beta_shift)
        start_state = jnp.zeros((key_in.shape[1], value_in.shape[1]), jnp.float32)
        final_state, outputs = run_blocks(queries, keys_unit, value_in, log_decay, betas, start_state, True)
        return jnp.sum(outputs * cot_rows)
    score_value, pull_back = jax.vjp(target_of, query_rows, key_rows, value_rows, decay_rows, beta_rows)
    return pull_back(jnp.ones_like(score_value))

def reference(tokens, step_index, embed_table, gain_one, gate_weight, up_weight, down_weight, gain_two, query_weight, key_weight, value_weight, decay_weight, beta_weight, rate_log, decay_bias, beta_bias, cotangent):
    embedded = jnp.take(embed_table, tokens, axis=0)
    emb_float = embedded.astype(jnp.float32)
    normed_one = rms_scaled(emb_float, gain_one).astype(jnp.bfloat16)
    gate_rows = jnp.dot(normed_one.astype(jnp.float32), gate_weight.astype(jnp.float32), preferred_element_type=jnp.float32)
    up_rows = jnp.dot(normed_one.astype(jnp.float32), up_weight.astype(jnp.float32), preferred_element_type=jnp.float32)
    hidden = jax.nn.silu(gate_rows) * up_rows
    path_scale = (step_index[0].astype(jnp.float32) + 0.5) / STEPS
    scaled = (path_scale * hidden).astype(jnp.bfloat16)
    group_units = FF // N_INNER
    mixed_rows = emb_float
    for member in range(N_INNER):
        first_unit = member * group_units
        last_unit = first_unit + group_units
        mixed_rows = mixed_rows + to_wire(jnp.dot(scaled[:, first_unit:last_unit].astype(jnp.float32), down_weight[first_unit:last_unit].astype(jnp.float32), preferred_element_type=jnp.float32))

    def normalize(values):
        return rms_scaled(values, gain_two)
    normed_float, norm_pull = jax.vjp(normalize, mixed_rows)
    normed_two = normed_float.astype(jnp.bfloat16)
    query_pre = jnp.dot(normed_two.astype(jnp.float32), query_weight.astype(jnp.float32), preferred_element_type=jnp.float32)
    key_pre = jnp.dot(normed_two.astype(jnp.float32), key_weight.astype(jnp.float32), preferred_element_type=jnp.float32)
    value_pre = jnp.dot(normed_two.astype(jnp.float32), value_weight.astype(jnp.float32), preferred_element_type=jnp.float32)
    decay_pre = jnp.dot(normed_two.astype(jnp.float32), decay_weight.astype(jnp.float32), preferred_element_type=jnp.float32)
    beta_pre = jnp.dot(normed_two.astype(jnp.float32), beta_weight.astype(jnp.float32), preferred_element_type=jnp.float32)

    def by_head(columns_block, width):
        return columns_block.reshape(TOKENS, H, width).transpose(1, 0, 2)
    cot_heads = by_head(cotangent.astype(jnp.float32), VD)
    gradients = lax.map(head_grads, (by_head(query_pre, KD), by_head(key_pre, KD), by_head(value_pre, VD), decay_pre.T, beta_pre.T, cot_heads, rate_log, decay_bias, beta_bias))

    def by_rows(head_block):
        return head_block.transpose(1, 0, 2).reshape(TOKENS, -1).astype(jnp.bfloat16)
    grad_query = by_rows(gradients[0])
    grad_key = by_rows(gradients[1])
    grad_value = by_rows(gradients[2])
    grad_decay = gradients[3].T.astype(jnp.bfloat16)
    grad_beta = gradients[4].T.astype(jnp.bfloat16)
    heads_dev = H // N_INNER
    back = jnp.zeros((TOKENS, D), jnp.float32)
    for member in range(N_INNER):
        key_lo = member * heads_dev * KD
        key_hi = key_lo + heads_dev * KD
        val_lo = member * heads_dev * VD
        val_hi = val_lo + heads_dev * VD
        head_lo = member * heads_dev
        head_hi = head_lo + heads_dev
        partial_sum = jnp.dot(grad_query[:, key_lo:key_hi].astype(jnp.float32), query_weight[:, key_lo:key_hi].T.astype(jnp.float32), preferred_element_type=jnp.float32)
        partial_sum = partial_sum + jnp.dot(grad_key[:, key_lo:key_hi].astype(jnp.float32), key_weight[:, key_lo:key_hi].T.astype(jnp.float32), preferred_element_type=jnp.float32)
        partial_sum = partial_sum + jnp.dot(grad_value[:, val_lo:val_hi].astype(jnp.float32), value_weight[:, val_lo:val_hi].T.astype(jnp.float32), preferred_element_type=jnp.float32)
        partial_sum = partial_sum + jnp.dot(grad_decay[:, head_lo:head_hi].astype(jnp.float32), decay_weight[:, head_lo:head_hi].T.astype(jnp.float32), preferred_element_type=jnp.float32)
        partial_sum = partial_sum + jnp.dot(grad_beta[:, head_lo:head_hi].astype(jnp.float32), beta_weight[:, head_lo:head_hi].T.astype(jnp.float32), preferred_element_type=jnp.float32)
        back = back + to_wire(partial_sum)
    grad_mixed = norm_pull(back)[0].astype(jnp.bfloat16)
    return hidden * jnp.dot(grad_mixed.astype(jnp.float32), down_weight.T.astype(jnp.float32), preferred_element_type=jnp.float32)
```

```python
import functools

import jax
import jax.numpy as jnp
from jax import lax
from jax.experimental import pallas as pl
from jax.experimental.pallas import tpu as pltpu
from jax.sharding import PartitionSpec as P

STEPS = 32
EPS = 1e-06
F32 = jnp.float32
BF16 = jnp.bfloat16
MESH = pl.DeviceIdType.MESH
HIGHEST = lax.Precision.HIGHEST
NN = (((1,), (0,)), ((), ()))
NT = (((1,), (1,)), ((), ()))
TN = (((0,), (0,)), ((), ()))


def exact(left, right, dims=NN):
    return lax.dot_general(left, right, dims, precision=HIGHEST, preferred_element_type=F32)


def fast(left, right, dims=NN):
    return lax.dot_general(
        left.astype(BF16), right.astype(BF16), dims, preferred_element_type=F32
    )


def row_sum(values):
    return jnp.sum(values, axis=1, keepdims=True)


def unit_inverse(lower, rows, cols):
    size = lower.shape[0]
    eye = (rows == cols).astype(F32)
    inverse, span = eye, 1
    while span < size:
        joined = (rows // (2 * span) == cols // (2 * span)) & (rows // span != cols // span)
        below = jnp.where(joined, lower, 0.0)
        if span == 1:
            inverse = eye - below
        else:
            inverse = inverse - exact(inverse, exact(below, inverse))
        span *= 2
    return inverse


def delta_prepare(query_pre, key_pre, values, decay_pre, beta_pre, cot, rate, decay_bias, beta_bias):
    size, key_dim = key_pre.shape
    query_inv = lax.rsqrt(row_sum(query_pre * query_pre) + EPS)
    key_inv = lax.rsqrt(row_sum(key_pre * key_pre) + EPS)
    queries = query_pre * (query_inv * key_dim ** (-0.5))
    keys = key_pre * key_inv
    shifted = decay_pre + decay_bias
    soft = jnp.maximum(shifted, 0.0) + jnp.log1p(jnp.exp(-jnp.abs(shifted)))
    log_decay = -jnp.exp(rate) * soft
    betas = 1.0 / (1.0 + jnp.exp(-(beta_pre + beta_bias)))

    rows = lax.broadcasted_iota(jnp.int32, (size, size), 0)
    cols = lax.broadcasted_iota(jnp.int32, (size, size), 1)
    lower = rows >= cols
    ones_lower = lower.astype(F32)
    cum_rows = exact(ones_lower, jnp.broadcast_to(log_decay, (size, size)))
    cum_cols = cum_rows.T
    ratio = jnp.where(lower, jnp.exp(jnp.where(lower, cum_rows - cum_cols, 0.0)), 0.0)
    cum = cum_rows[:, 0:1]
    cum_last = cum_cols[:, size - 1 : size]
    grown = jnp.exp(cum)
    left_over = jnp.exp(cum_last - cum)
    total = jnp.exp(cum_last[0:1, :])

    key_gram = exact(keys, keys, NT)
    ratio_gram = jnp.where(rows > cols, ratio * key_gram, 0.0)
    strict = betas * ratio_gram
    inverse = unit_inverse(strict, rows, cols)
    scores = ratio * exact(queries, keys, NT)
    keys_grown = grown * keys
    queries_grown = grown * queries
    keys_tail = left_over * keys

    fresh_free = exact(inverse, betas * values)
    fresh_map = exact(inverse, betas * keys_grown)
    back_free = exact(inverse, exact(scores, cot, TN), TN)
    back_map = exact(inverse, keys_tail, TN)
    eye = (
        lax.broadcasted_iota(jnp.int32, (key_dim, key_dim), 0)
        == lax.broadcasted_iota(jnp.int32, (key_dim, key_dim), 1)
    ).astype(F32)
    transition = total * eye - exact(keys_tail, fresh_map, TN)
    transition_back = total * eye - exact(fresh_map, keys_tail, TN)
    offset = exact(keys_tail, fresh_free, TN)
    offset_back = exact(queries_grown, cot, TN) - exact(betas * keys_grown, back_free, TN)
    kept = dict(
        query_pre=query_pre, key_pre=key_pre, values=values, query_inv=query_inv, key_inv=key_inv,
        queries=queries, keys=keys, shifted=shifted, betas=betas, ratio=ratio, grown=grown,
        left_over=left_over, total=total, ratio_gram=ratio_gram, strict=strict, scores=scores,
        keys_grown=keys_grown, keys_tail=keys_tail, fresh_free=fresh_free, fresh_map=fresh_map,
        back_free=back_free, back_map=back_map, cot=cot, rate=rate,
    )
    return kept, (transition, offset), (transition_back, offset_back)


def delta_finish(kept, state, end_grad):
    k = kept
    size, key_dim = k["keys"].shape
    scale = key_dim ** (-0.5)
    rows = lax.broadcasted_iota(jnp.int32, (size, size), 0)
    cols = lax.broadcasted_iota(jnp.int32, (size, size), 1)
    fresh = k["fresh_free"] - exact(k["fresh_map"], state)
    back = k["back_free"] + exact(k["back_map"], end_grad)
    d_strict = jnp.where(rows > cols, -exact(back, fresh, NT), 0.0)
    d_gram = d_strict * (k["betas"] * k["ratio"])
    d_scores = exact(k["cot"], fresh, NT) * k["ratio"]
    residual = k["values"] - exact(k["keys_grown"], state)
    d_values = k["betas"] * back
    d_betas = row_sum(back * residual) + row_sum(d_strict * k["ratio_gram"])
    cot_state = k["grown"] * exact(k["cot"], state, NT)
    back_state = (k["grown"] * k["betas"]) * exact(back, state, NT)
    fresh_end = k["left_over"] * exact(fresh, end_grad, NT)
    d_queries = exact(d_scores, k["keys"]) + cot_state
    d_keys_read = exact(d_gram, k["keys"]) - back_state
    d_keys_write = exact(d_gram, k["keys"], TN) + exact(d_scores, k["queries"], TN) + fresh_end
    d_cum = row_sum(k["queries"] * d_queries) + row_sum(k["keys"] * (d_keys_read - d_keys_write))
    ends = jnp.sum(row_sum(k["keys"] * fresh_end), axis=0, keepdims=True) + k["total"] * jnp.sum(
        row_sum(state * end_grad), axis=0, keepdims=True
    )
    upper = (rows <= cols).astype(F32)
    d_log = exact(upper, jnp.broadcast_to(d_cum, (size, key_dim)))[:, 0:1] + ends

    query_inv, key_inv = k["query_inv"], k["key_inv"]
    d_query = (scale * query_inv) * (
        d_queries - k["query_pre"] * (query_inv * query_inv * row_sum(k["query_pre"] * d_queries))
    )
    d_keys = d_keys_read + d_keys_write
    d_key = key_inv * (d_keys - k["keys"] * row_sum(k["keys"] * d_keys))
    d_decay = d_log * (-jnp.exp(k["rate"])) * (1.0 / (1.0 + jnp.exp(-k["shifted"])))
    d_beta = d_betas * k["betas"] * (1.0 - k["betas"])
    return d_query, d_key, d_values, d_decay, d_beta


def kernel(
    chips, turn_of,
    columns_ref, step_ref, rate_ref, decay_bias_ref, beta_bias_ref, gain_one_ref, gain_two_ref,
    decay_ref, beta_ref, gate_hbm, up_hbm, down_hbm, query_hbm, key_hbm, value_hbm, cot_hbm,
    out_ref,
    gate_w, up_w, down_w, main_w, cot_v, gates_w, emb, normed, hidden, part, heap_one, heap_two,
    normed_two, grad_mixed, mixed_own, state_own, pair_map_out, pair_map_in, pair_off_out,
    pair_off_in, carry_in, carry_out, share_out, share_in,
    load_sem, send_sem, recv_sem, side_send, side_recv,
):
    me = lax.axis_index("inner")
    outer = lax.axis_index("outer")
    peers = lax.axis_size("inner")
    chip, core = outer // 2, lax.rem(outer, 2)
    partner = {"outer": outer + 1 - 2 * core}
    ahead = {"outer": lax.rem(chip + 1, chips) * 2 + core}
    behind = {"outer": lax.rem(chip + chips - 1, chips) * 2 + core}
    turn = chip + core * (chips - 1 - 2 * chip)
    onward = {"outer": lax.rem(chip + chips + 1 - 2 * core, chips) * 2 + core}

    key_dim = query_hbm.shape[1]
    value_dim = value_hbm.shape[1]
    width = down_hbm.shape[1]
    rows = columns_ref.shape[0]
    share = rows // peers
    slab = columns_ref.shape[1]

    loads = [
        pltpu.make_async_copy(gate_hbm, gate_w, load_sem.at[0]),
        pltpu.make_async_copy(up_hbm, up_w, load_sem.at[1]),
        pltpu.make_async_copy(down_hbm, down_w, load_sem.at[2]),
        pltpu.make_async_copy(query_hbm, main_w.at[:, pl.ds(0, key_dim)], load_sem.at[3]),
        pltpu.make_async_copy(key_hbm, main_w.at[:, pl.ds(key_dim, key_dim)], load_sem.at[4]),
        pltpu.make_async_copy(value_hbm, main_w.at[:, pl.ds(2 * key_dim, value_dim)], load_sem.at[5]),
        pltpu.make_async_copy(cot_hbm, cot_v, load_sem.at[6]),
    ]
    own_cols = pl.ds(pl.multiple_of(me * slab, slab), slab)
    own_rows = pl.ds(pl.multiple_of(me * share, share), share)
    place = pltpu.make_async_copy(columns_ref, emb.at[:, own_cols], load_sem.at[7])
    place.start()
    for load in loads:
        load.start()

    barrier = pltpu.get_barrier_semaphore()
    for step in range(1, peers):
        pl.semaphore_signal(
            barrier, inc=1, device_id={"inner": lax.rem(me + step, peers)}, device_id_type=MESH
        )
    for side in (partner, ahead, behind):
        pl.semaphore_signal(barrier, inc=1, device_id=side, device_id_type=MESH)
    pl.semaphore_wait(barrier, peers + 2)

    def to_peers(stage, source, target):
        copies = []
        for step in range(1, peers):
            peer = lax.rem(me + step, peers)
            copy = pltpu.make_async_remote_copy(
                src_ref=source(peer),
                dst_ref=target(step),
                send_sem=send_sem.at[stage, step - 1],
                recv_sem=recv_sem.at[stage, step - 1],
                device_id={"inner": peer},
                device_id_type=MESH,
            )
            copy.start()
            copies.append(copy)
        return copies

    def rows_of(owner):
        return pl.ds(pl.multiple_of(owner * share, share), share)

    copies = to_peers(0, lambda peer: columns_ref, lambda step: emb.at[:, own_cols])
    row_id = lax.broadcasted_iota(jnp.int32, (8, width), 0)
    gates_w[...] = jnp.where(
        row_id == 0,
        decay_ref[...].astype(F32),
        jnp.where(row_id == 1, beta_ref[...].astype(F32), 0.0),
    )
    place.wait()
    for copy in copies:
        copy.wait()

    def norm_one(index, carry):
        at = pl.ds(pl.multiple_of(index * 16, 16), 16)
        values = emb[at, :].astype(F32)
        scale = lax.rsqrt(row_sum(values * values) * (1.0 / width) + EPS)
        normed[at, :] = (values * scale * gain_one_ref[...]).astype(BF16)
        return carry

    lax.fori_loop(0, rows // 16, norm_one, 0)
    loads[0].wait()
    loads[1].wait()
    gate_rows = jnp.dot(normed[...], gate_w[...], preferred_element_type=F32)
    up_rows = jnp.dot(normed[...], up_w[...], preferred_element_type=F32)
    active = gate_rows * (1.0 / (1.0 + jnp.exp(-gate_rows))) * up_rows
    hidden[...] = active
    path_scale = (step_ref[...].astype(F32) + 0.5) / STEPS
    scaled = (path_scale * active).astype(BF16)
    loads[2].wait()
    for piece in range(width // 256):
        at = slice(piece * 256, piece * 256 + 256)
        part[:, at] = jnp.dot(scaled, down_w[:, at], preferred_element_type=F32).astype(BF16)

    def reduce_rows(stage, heap):
        copies = to_peers(stage, lambda peer: part.at[rows_of(peer), :], lambda step: heap.at[step - 1])
        acc = part[own_rows, :].astype(F32)
        for step, copy in enumerate(copies):
            copy.wait()
            acc = acc + heap[step].astype(F32)
        return acc

    mixed = emb[own_rows, :].astype(F32) + reduce_rows(1, heap_one)
    mixed_own[...] = mixed
    inv_two = lax.rsqrt(row_sum(mixed * mixed) * (1.0 / width) + EPS)
    normed_two[own_rows, :] = (mixed * inv_two * gain_two_ref[...]).astype(BF16)

    def spread_rows(stage, array):
        copies = to_peers(stage, lambda peer: array.at[own_rows, :], lambda step: array.at[own_rows, :])
        for copy in copies:
            copy.wait()

    spread_rows(2, normed_two)
    for load in loads[3:]:
        load.wait()
    main = jnp.dot(normed_two[...], main_w[...], preferred_element_type=F32)
    gates = lax.dot_general(
        normed_two[...], gates_w[...].astype(BF16), NT, preferred_element_type=F32
    )
    kept, ahead_map, back_map = delta_prepare(
        main[:, :key_dim],
        main[:, key_dim : 2 * key_dim],
        main[:, 2 * key_dim :],
        gates[:, 0:1],
        gates[:, 1:2],
        cot_v[...].astype(F32),
        rate_ref[...],
        decay_bias_ref[...],
        beta_bias_ref[...],
    )

    first = core == 0
    own_map = jnp.where(first, ahead_map[0], back_map[0])
    own_off = jnp.where(first, ahead_map[1], back_map[1])
    pair_map_out[...] = jnp.where(first, back_map[0], ahead_map[0])
    pair_off_out[...] = jnp.where(first, back_map[1], ahead_map[1]).astype(BF16)

    def to_side(index, source, target, device):
        return pltpu.make_async_remote_copy(
            src_ref=source,
            dst_ref=target,
            send_sem=side_send.at[index],
            recv_sem=side_recv.at[index],
            device_id=device,
            device_id_type=MESH,
        )

    pair_copies = [
        to_side(0, pair_map_out, pair_map_in, partner),
        to_side(1, pair_off_out, pair_off_in, partner),
    ]
    for copy in pair_copies:
        copy.start()
    for copy in pair_copies:
        copy.wait()
    chip_map = exact(pair_map_in[...], own_map)
    chip_off = exact(pair_map_in[...], own_off) + pair_off_in[...].astype(F32)

    pass_on = to_side(2, carry_out, carry_in, onward)

    @pl.when(turn == 0)
    def _():
        carry_in[...] = jnp.zeros_like(carry_in)

    @pl.when(turn > 0)
    def _():
        pass_on.wait_recv()

    @pl.when(turn < chips - 1)
    def _():
        carry_out[...] = (exact(chip_map, carry_in[...].astype(F32)) + chip_off).astype(BF16)
        pass_on.start()

    carried = carry_in[...].astype(F32)
    share_out[...] = (exact(own_map, carried) + own_off).astype(BF16)
    swap = to_side(3, share_out, share_in, partner)
    swap.start()
    swap.wait()
    other = share_in[...].astype(F32)
    state = jnp.where(first, carried, other)
    end_grad = jnp.where(first, other, carried)
    d_query, d_key, d_value, d_decay, d_beta = delta_finish(kept, state, end_grad)

    @pl.when(turn < chips - 1)
    def _():
        pass_on.wait_send()

    grads = jnp.concatenate([d_query, d_key, d_value], axis=1).astype(BF16)
    d_decay = d_decay.astype(BF16).astype(F32)
    d_beta = d_beta.astype(BF16).astype(F32)
    for piece in range(width // 256):
        at = slice(piece * 256, piece * 256 + 256)
        back = lax.dot_general(grads, main_w[at, :], NT, preferred_element_type=F32)
        back = back + d_decay * gates_w[0:1, at] + d_beta * gates_w[1:2, at]
        part[:, at] = back.astype(BF16)
    back = reduce_rows(3, heap_two)
    mixed = mixed_own[...]
    inv_two = lax.rsqrt(row_sum(mixed * mixed) * (1.0 / width) + EPS)
    gained = back * gain_two_ref[...]
    inner_sum = row_sum(mixed * gained) * (1.0 / width)
    grad_mixed[own_rows, :] = (
        inv_two * gained - mixed * (inv_two * inv_two * inv_two * inner_sum)
    ).astype(BF16)
    spread_rows(4, grad_mixed)
    out_ref[...] = hidden[...] * lax.dot_general(
        grad_mixed[...], down_w[...], NT, preferred_element_type=F32
    )


def shards(
    tokens, step_index, embed_table, gain_one, gate_weight, up_weight, down_weight, gain_two,
    query_weight, key_weight, value_weight, decay_weight, beta_weight, rate_log, decay_bias,
    beta_bias, cotangent,
):
    columns = embed_table.at[tokens].get(mode="promise_in_bounds")
    peers = lax.axis_size("inner")
    chips = lax.axis_size("outer") // 2
    rows, slab = columns.shape
    width = slab * peers
    hidden_dim = gate_weight.shape[1]
    key_dim, value_dim = query_weight.shape[1], value_weight.shape[1]
    share = rows // peers
    in_vmem = pl.BlockSpec(memory_space=pltpu.VMEM)
    in_place = pl.BlockSpec(memory_space=pl.ANY)
    vm = pltpu.VMEM
    return pl.pallas_call(
        functools.partial(kernel, chips, None),
        out_shape=jax.ShapeDtypeStruct((rows, hidden_dim), F32),
        in_specs=[in_vmem] * 9 + [in_place] * 7,
        out_specs=in_vmem,
        scratch_shapes=[
            vm((width, hidden_dim), BF16),
            vm((width, hidden_dim), BF16),
            vm((hidden_dim, width), BF16),
            vm((width, 2 * key_dim + value_dim), BF16),
            vm((rows, value_dim), BF16),
            vm((8, width), F32),
            vm((rows, width), BF16),
            vm((rows, width), BF16),
            vm((rows, hidden_dim), F32),
            vm((rows, width), BF16),
            vm((peers - 1, share, width), BF16),
            vm((peers - 1, share, width), BF16),
            vm((rows, width), BF16),
            vm((rows, width), BF16),
            vm((share, width), F32),
            vm((key_dim, value_dim), F32),
            vm((key_dim, key_dim), F32),
            vm((key_dim, key_dim), F32),
            vm((key_dim, value_dim), BF16),
            vm((key_dim, value_dim), BF16),
            vm((key_dim, value_dim), BF16),
            vm((key_dim, value_dim), BF16),
            vm((key_dim, value_dim), BF16),
            vm((key_dim, value_dim), BF16),
            pltpu.SemaphoreType.DMA((8,)),
            pltpu.SemaphoreType.DMA((5, peers - 1)),
            pltpu.SemaphoreType.DMA((5, peers - 1)),
            pltpu.SemaphoreType.DMA((4,)),
            pltpu.SemaphoreType.DMA((4,)),
        ],
        compiler_params=pltpu.CompilerParams(collective_id=0, has_side_effects=True),
        name="attribution",
    )(
        columns,
        step_index.reshape(1, 1),
        rate_log.reshape(1, 1),
        decay_bias.reshape(1, 1),
        beta_bias.reshape(1, 1),
        gain_one.reshape(1, width),
        gain_two.reshape(1, width),
        decay_weight.reshape(1, width),
        beta_weight.reshape(1, width),
        gate_weight,
        up_weight,
        down_weight,
        query_weight,
        key_weight,
        value_weight,
        cotangent,
    )


def solution(mesh):
    placed = (
        P("outer"), P(), P(None, "inner"), P(), P(None, "inner"), P(None, "inner"),
        P("inner", None), P(), P(None, "inner"), P(None, "inner"), P(None, "inner"),
        P(None, "inner"), P(None, "inner"), P("inner"), P("inner"), P("inner"),
        P("outer", "inner"),
    )
    return jax.shard_map(
        shards, mesh=mesh, in_specs=placed, out_specs=P("outer", "inner"), check_vma=False
    )
```

```python
import functools

import jax
import jax.numpy as jnp
from jax import lax
from jax.experimental import pallas as pl
from jax.experimental.pallas import tpu as pltpu
from jax.sharding import PartitionSpec as P

STEPS = 32
EPS = 1e-06
F32 = jnp.float32
BF16 = jnp.bfloat16
MESH = pl.DeviceIdType.MESH
HIGHEST = lax.Precision.HIGHEST
NN = (((1,), (0,)), ((), ()))
NT = (((1,), (1,)), ((), ()))
TN = (((0,), (0,)), ((), ()))


def exact(left, right, dims=NN):
    return lax.dot_general(left, right, dims, precision=HIGHEST, preferred_element_type=F32)


def fast(left, right, dims=NN):
    return lax.dot_general(
        left.astype(BF16), right.astype(BF16), dims, preferred_element_type=F32
    )


def row_sum(values):
    return jnp.sum(values, axis=1, keepdims=True)


def split(value):
    high = value.astype(BF16)
    return high, (value - high.astype(F32)).astype(BF16)


def triple(left, right, dims=NN):
    left_high, left_low = split(left)
    right_high, right_low = split(right)

    def dot(one, two):
        return lax.dot_general(one, two, dims, preferred_element_type=F32)

    return dot(left_high, right_high) + (dot(left_high, right_low) + dot(left_low, right_high))


near = triple
solve = triple
gram = triple


def unit_inverse(lower, rows, cols):
    size = lower.shape[0]
    eye = (rows == cols).astype(F32)
    inverse, span = eye, 1
    while span < size:
        joined = (rows // (2 * span) == cols // (2 * span)) & (rows // span != cols // span)
        below = jnp.where(joined, lower, 0.0)
        if span == 1:
            inverse = eye - below
        else:
            inverse = inverse - solve(inverse, solve(below, inverse))
        span *= 2
    return inverse


def delta_prepare(query_pre, key_pre, values, decay_pre, beta_pre, cot, rate, decay_bias, beta_bias):
    size, key_dim = key_pre.shape
    query_inv = lax.rsqrt(row_sum(query_pre * query_pre) + EPS)
    key_inv = lax.rsqrt(row_sum(key_pre * key_pre) + EPS)
    queries = query_pre * (query_inv * key_dim ** (-0.5))
    keys = key_pre * key_inv
    shifted = decay_pre + decay_bias
    soft = jnp.maximum(shifted, 0.0) + jnp.log1p(jnp.exp(-jnp.abs(shifted)))
    log_decay = -jnp.exp(rate) * soft
    betas = 1.0 / (1.0 + jnp.exp(-(beta_pre + beta_bias)))

    rows = lax.broadcasted_iota(jnp.int32, (size, size), 0)
    cols = lax.broadcasted_iota(jnp.int32, (size, size), 1)
    lower = rows >= cols
    ones_lower = lower.astype(F32)
    cum_rows = exact(ones_lower, jnp.broadcast_to(log_decay, (size, size)))
    cum_cols = cum_rows.T
    ratio = jnp.where(lower, jnp.exp(jnp.where(lower, cum_rows - cum_cols, 0.0)), 0.0)
    cum = cum_rows[:, 0:1]
    cum_last = cum_cols[:, size - 1 : size]
    grown = jnp.exp(cum)
    left_over = jnp.exp(cum_last - cum)
    total = jnp.exp(cum_last[0:1, :])

    key_gram = gram(keys, keys, NT)
    ratio_gram = jnp.where(rows > cols, ratio * key_gram, 0.0)
    strict = betas * ratio_gram
    inverse = unit_inverse(strict, rows, cols)
    scores = ratio * near(queries, keys, NT)
    keys_grown = grown * keys
    queries_grown = grown * queries
    keys_tail = left_over * keys

    fresh_free = near(inverse, betas * values)
    fresh_map = near(inverse, betas * keys_grown)
    back_free = near(inverse, near(scores, cot, TN), TN)
    back_map = near(inverse, keys_tail, TN)
    eye = (
        lax.broadcasted_iota(jnp.int32, (key_dim, key_dim), 0)
        == lax.broadcasted_iota(jnp.int32, (key_dim, key_dim), 1)
    ).astype(F32)
    transition = total * eye - near(keys_tail, fresh_map, TN)
    transition_back = total * eye - near(fresh_map, keys_tail, TN)
    offset = near(keys_tail, fresh_free, TN)
    offset_back = near(queries_grown, cot, TN) - near(betas * keys_grown, back_free, TN)
    kept = dict(
        query_pre=query_pre, key_pre=key_pre, values=values, query_inv=query_inv, key_inv=key_inv,
        queries=queries, keys=keys, shifted=shifted, betas=betas, ratio=ratio, grown=grown,
        left_over=left_over, total=total, ratio_gram=ratio_gram, strict=strict, scores=scores,
        keys_grown=keys_grown, keys_tail=keys_tail, fresh_free=fresh_free, fresh_map=fresh_map,
        back_free=back_free, back_map=back_map, cot=cot, rate=rate,
    )
    return kept, (transition, offset), (transition_back, offset_back)


def delta_finish(kept, state, end_grad):
    k = kept
    size, key_dim = k["keys"].shape
    scale = key_dim ** (-0.5)
    rows = lax.broadcasted_iota(jnp.int32, (size, size), 0)
    cols = lax.broadcasted_iota(jnp.int32, (size, size), 1)
    fresh = k["fresh_free"] - near(k["fresh_map"], state)
    back = k["back_free"] + near(k["back_map"], end_grad)
    d_strict = jnp.where(rows > cols, -near(back, fresh, NT), 0.0)
    d_gram = d_strict * (k["betas"] * k["ratio"])
    d_scores = near(k["cot"], fresh, NT) * k["ratio"]
    residual = k["values"] - near(k["keys_grown"], state)
    d_values = k["betas"] * back
    d_betas = row_sum(back * residual) + row_sum(d_strict * k["ratio_gram"])
    cot_state = k["grown"] * near(k["cot"], state, NT)
    back_state = (k["grown"] * k["betas"]) * near(back, state, NT)
    fresh_end = k["left_over"] * near(fresh, end_grad, NT)
    d_queries = near(d_scores, k["keys"]) + cot_state
    d_keys_read = near(d_gram, k["keys"]) - back_state
    d_keys_write = near(d_gram, k["keys"], TN) + near(d_scores, k["queries"], TN) + fresh_end
    d_cum = row_sum(k["queries"] * d_queries) + row_sum(k["keys"] * (d_keys_read - d_keys_write))
    ends = jnp.sum(row_sum(k["keys"] * fresh_end), axis=0, keepdims=True) + k["total"] * jnp.sum(
        row_sum(state * end_grad), axis=0, keepdims=True
    )
    upper = (rows <= cols).astype(F32)
    d_log = exact(upper, jnp.broadcast_to(d_cum, (size, key_dim)))[:, 0:1] + ends

    query_inv, key_inv = k["query_inv"], k["key_inv"]
    d_query = (scale * query_inv) * (
        d_queries - k["query_pre"] * (query_inv * query_inv * row_sum(k["query_pre"] * d_queries))
    )
    d_keys = d_keys_read + d_keys_write
    d_key = key_inv * (d_keys - k["keys"] * row_sum(k["keys"] * d_keys))
    d_decay = d_log * (-jnp.exp(k["rate"])) * (1.0 / (1.0 + jnp.exp(-k["shifted"])))
    d_beta = d_betas * k["betas"] * (1.0 - k["betas"])
    return d_query, d_key, d_values, d_decay, d_beta


def ring_order(side):
    return sorted(range(1, side), key=lambda step: (-min(step, side - step), step))


def kernel(
    chips,
    tokens_ref, step_ref, rate_ref, decay_bias_ref, beta_bias_ref, gain_one_ref, gain_two_ref,
    decay_ref, beta_ref, table_hbm, gate_hbm, up_hbm, down_hbm, query_hbm, key_hbm, value_hbm,
    cot_hbm,
    out_ref,
    table, gate_w, up_w, down_w, main_w, cot_v, gates_w, emb, normed, hidden, part,
    heap_one, heap_two, sums, last_one, last_two,
    normed_two, grad_mixed, mixed_own, pair_map_out, pair_map_in, pair_off_out,
    pair_off_in, carry_in, carry_out, share_out, share_in,
    load_sem, send_sem, recv_sem, side_send, side_recv,
):
    me = lax.axis_index("inner")
    outer = lax.axis_index("outer")
    peers = lax.axis_size("inner")
    side = int(round(peers**0.5))
    line, spot = me // side, lax.rem(me, side)
    chip, core = outer // 2, lax.rem(outer, 2)
    partner = {"outer": outer + 1 - 2 * core}
    ahead = {"outer": lax.rem(chip + 1, chips) * 2 + core}
    behind = {"outer": lax.rem(chip + chips - 1, chips) * 2 + core}
    turn = chip + core * (chips - 1 - 2 * chip)
    onward = {"outer": lax.rem(chip + chips + 1 - 2 * core, chips) * 2 + core}

    key_dim = query_hbm.shape[1]
    value_dim = value_hbm.shape[1]
    width = down_hbm.shape[1]
    half = width // 2
    rows = tokens_ref.shape[0]
    share = rows // peers
    slab = table.shape[2]

    loads = [
        pltpu.make_async_copy(gate_hbm, gate_w, load_sem.at[0]),
        pltpu.make_async_copy(up_hbm, up_w, load_sem.at[1]),
        pltpu.make_async_copy(down_hbm, down_w, load_sem.at[2]),
        pltpu.make_async_copy(query_hbm, main_w.at[:, pl.ds(0, key_dim)], load_sem.at[3]),
        pltpu.make_async_copy(key_hbm, main_w.at[:, pl.ds(key_dim, key_dim)], load_sem.at[4]),
        pltpu.make_async_copy(value_hbm, main_w.at[:, pl.ds(2 * key_dim, value_dim)], load_sem.at[5]),
        pltpu.make_async_copy(cot_hbm, cot_v, load_sem.at[6]),
    ]
    table_load = pltpu.make_async_copy(table_hbm, table, load_sem.at[7])
    table_load.start()

    barrier = pltpu.get_barrier_semaphore()
    for step in range(1, side):
        for peer in (
            lax.rem(line + step, side) * side + spot,
            line * side + lax.rem(spot + step, side),
        ):
            pl.semaphore_signal(barrier, inc=1, device_id={"inner": peer}, device_id_type=MESH)
    for device in (partner, ahead, behind):
        pl.semaphore_signal(barrier, inc=1, device_id=device, device_id_type=MESH)
    for load in loads:
        load.start()

    row_id = lax.broadcasted_iota(jnp.int32, (8, width), 0)
    gates_w[...] = jnp.where(
        row_id == 0,
        decay_ref[...].astype(F32),
        jnp.where(row_id == 1, beta_ref[...].astype(F32), 0.0),
    )

    table_load.wait()
    tile_row = lax.broadcasted_iota(jnp.int32, (8, slab), 0)

    def pick(index, carry):
        found = []
        for part_of in range(2):
            tile = jnp.zeros((8, slab), F32)
            for row in range(8):
                token = tokens_ref[index * 16 + part_of * 8 + row]
                near_rows = table[lax.shift_right_logical(token, 3)].astype(F32)
                chosen = jnp.sum(
                    jnp.where(tile_row == (token & 7), near_rows, 0.0), axis=0, keepdims=True
                )
                tile = jnp.where(tile_row == row, chosen, tile)
            found.append(tile)
        emb[me, pl.ds(pl.multiple_of(index * 16, 16), 16), :] = jnp.concatenate(
            found, axis=0
        ).astype(BF16)
        return carry

    lax.fori_loop(0, rows // 16, pick, 0)
    pl.semaphore_wait(barrier, 2 * (side - 1) + 3)

    def to_axis(across, step):
        if across:
            return line * side + lax.rem(spot + step, side)
        return lax.rem(line + step, side) * side + spot

    def send(stage, way, index, source, target, peer):
        copy = pltpu.make_async_remote_copy(
            src_ref=source,
            dst_ref=target,
            send_sem=send_sem.at[stage, way, index],
            recv_sem=recv_sem.at[stage, way, index],
            device_id={"inner": peer},
            device_id_type=MESH,
        )
        copy.start()
        return copy

    order = ring_order(side)

    def spread(stage, piece):
        first_hop, second_hop = [{}, {}], []
        for step in order:
            for way in range(2):
                own = piece(me, way)
                first_hop[way][step] = send(stage, way, step - 1, own, own, to_axis(way, step))
        for step in order:
            for way in range(2):
                own = piece(me, way)
                second_hop.append(
                    send(stage, way, side - 1 + step - 1, own, own, to_axis(1 - way, step))
                )
        for gone in reversed(order):
            for way in range(2):
                first_hop[way][gone].wait_recv()
                got = piece(to_axis(way, side - gone), way)
                for step in order:
                    index = (side - 1) * (1 + gone) + step - 1
                    second_hop.append(send(stage, way, index, got, got, to_axis(1 - way, step)))
        for copy in second_hop:
            copy.wait()
        for way in range(2):
            for step in order:
                first_hop[way][step].wait_send()

    def reduce_send(stage, heap, way):
        hops = {}
        for apart in order + [0]:
            for step in order:
                if way == 0:
                    at = (lax.rem(line + apart, side), lax.rem(spot + step, side))
                else:
                    at = (lax.rem(line + step, side), lax.rem(spot + apart, side))
                index = apart * (side - 1) + step - 1
                hops[apart, step] = send(
                    stage, way, index, part.at[way, at[0], at[1]], heap.at[way, index],
                    to_axis(1 - way, step),
                )
        return hops

    def reduce_finish(stage, heap, last, hops):
        own, second_hop = [None, None], [[], []]
        for apart in order + [0]:
            for way in range(2):
                if way == 0:
                    at = (lax.rem(line + apart, side), spot)
                else:
                    at = (line, lax.rem(spot + apart, side))
                total = part[way, at[0], at[1]].astype(F32)
                for step in reversed(order):
                    hops[way][apart, step].wait_recv()
                    total = total + heap[way, apart * (side - 1) + step - 1].astype(F32)
                if apart == 0:
                    own[way] = total
                else:
                    sums[way, apart - 1] = total.astype(BF16)
                    second_hop[way].append(
                        (apart, send(
                            stage, way, side * (side - 1) + apart - 1, sums.at[way, apart - 1],
                            last.at[way, apart - 1], to_axis(way, apart),
                        ))
                    )
        for way in range(2):
            for apart, copy in second_hop[way]:
                copy.wait()
                own[way] = own[way] + last[way, apart - 1].astype(F32)
            for copy in hops[way].values():
                copy.wait_send()
        return jnp.concatenate(own, axis=1)

    spread(0, lambda owner, way: emb.at[owner, pl.ds(way * (rows // 2), rows // 2), :])

    def norm_one(index, carry):
        at = pl.ds(pl.multiple_of(index * 16, 16), 16)
        values = [emb[owner, at, :].astype(F32) for owner in range(peers)]
        squares = values[0] * values[0]
        for value in values[1:]:
            squares = squares + value * value
        scale = lax.rsqrt(row_sum(squares) * (1.0 / width) + EPS)
        for owner, value in enumerate(values):
            cut = slice(owner * slab, (owner + 1) * slab)
            normed[at, cut] = (value * scale * gain_one_ref[:, cut]).astype(BF16)
        return carry

    lax.fori_loop(0, rows // 16, norm_one, 0, unroll=2)
    loads[0].wait()
    loads[1].wait()
    gate_rows = lax.dot_general(normed[...], gate_w[...], NT, preferred_element_type=F32)
    up_rows = lax.dot_general(normed[...], up_w[...], NT, preferred_element_type=F32)
    active = gate_rows * (1.0 / (1.0 + jnp.exp(-gate_rows))) * up_rows
    path_scale = (step_ref[...].astype(F32) + 0.5) / STEPS
    scaled = (path_scale * active).astype(BF16)
    loads[2].wait()

    def partial_half(way, product):
        for first in range(way * half, way * half + half, 256):
            block = product(slice(first, first + 256)).astype(BF16)
            at = slice(first - way * half, first - way * half + 256)
            part[way, :, :, :, at] = block.reshape(side, side, share, 256)

    hops = []
    for way in range(2):
        partial_half(
            way, lambda at: jnp.dot(scaled, down_w[:, at], preferred_element_type=F32)
        )
        hops.append(reduce_send(1, heap_one, way))
    hidden[...] = active.T
    own_rows = pl.ds(pl.multiple_of(me * share, share), share)
    own_emb = jnp.concatenate([emb[owner, own_rows, :] for owner in range(peers)], axis=1)
    mixed = own_emb.astype(F32) + reduce_finish(1, heap_one, last_one, hops)
    mixed_own[...] = mixed
    inv_two = lax.rsqrt(row_sum(mixed * mixed) * (1.0 / width) + EPS)
    normed_two[own_rows, :] = (mixed * inv_two * gain_two_ref[...]).astype(BF16)

    def row_piece(array):
        return lambda owner, way: array.at[
            pl.ds(pl.multiple_of(owner * share, share), share), pl.ds(way * half, half)
        ]

    spread(2, row_piece(normed_two))
    for load in loads[3:]:
        load.wait()
    main = jnp.dot(normed_two[...], main_w[...], preferred_element_type=F32)
    gates = lax.dot_general(
        normed_two[...], gates_w[...].astype(BF16), NT, preferred_element_type=F32
    )
    kept, ahead_map, back_map = delta_prepare(
        main[:, :key_dim],
        main[:, key_dim : 2 * key_dim],
        main[:, 2 * key_dim :],
        gates[:, 0:1],
        gates[:, 1:2],
        cot_v[...].astype(F32),
        rate_ref[...],
        decay_bias_ref[...],
        beta_bias_ref[...],
    )

    first = core == 0
    own_map = jnp.where(first, ahead_map[0], back_map[0])
    own_off = jnp.where(first, ahead_map[1], back_map[1])
    pair_map_out[...] = jnp.where(first, back_map[0], ahead_map[0])
    pair_off_out[...] = jnp.where(first, back_map[1], ahead_map[1]).astype(BF16)

    def to_side(index, source, target, device):
        return pltpu.make_async_remote_copy(
            src_ref=source,
            dst_ref=target,
            send_sem=side_send.at[index],
            recv_sem=side_recv.at[index],
            device_id=device,
            device_id_type=MESH,
        )

    pair_copies = [
        to_side(0, pair_map_out, pair_map_in, partner),
        to_side(1, pair_off_out, pair_off_in, partner),
    ]
    for copy in pair_copies:
        copy.start()
    for copy in pair_copies:
        copy.wait()
    chip_map = exact(pair_map_in[...], own_map)
    chip_off = exact(pair_map_in[...], own_off) + pair_off_in[...].astype(F32)

    pass_on = to_side(2, carry_out, carry_in, onward)

    @pl.when(turn == 0)
    def _():
        carry_in[...] = jnp.zeros_like(carry_in)

    @pl.when(turn > 0)
    def _():
        pass_on.wait_recv()

    @pl.when(turn < chips - 1)
    def _():
        carry_out[...] = (exact(chip_map, carry_in[...].astype(F32)) + chip_off).astype(BF16)
        pass_on.start()

    carried = carry_in[...].astype(F32)
    share_out[...] = (exact(own_map, carried) + own_off).astype(BF16)
    swap = to_side(3, share_out, share_in, partner)
    swap.start()
    swap.wait()
    other = share_in[...].astype(F32)
    state = jnp.where(first, carried, other)
    end_grad = jnp.where(first, other, carried)
    d_query, d_key, d_value, d_decay, d_beta = delta_finish(kept, state, end_grad)

    @pl.when(turn < chips - 1)
    def _():
        pass_on.wait_send()

    grads = jnp.concatenate([d_query, d_key, d_value], axis=1).astype(BF16)
    d_decay = d_decay.astype(BF16).astype(F32)
    d_beta = d_beta.astype(BF16).astype(F32)

    def back_block(at):
        block = lax.dot_general(grads, main_w[at, :], NT, preferred_element_type=F32)
        return block + d_decay * gates_w[0:1, at] + d_beta * gates_w[1:2, at]

    hops = []
    for way in range(2):
        partial_half(way, back_block)
        hops.append(reduce_send(3, heap_two, way))
    back = reduce_finish(3, heap_two, last_two, hops)
    mixed = mixed_own[...]
    inv_two = lax.rsqrt(row_sum(mixed * mixed) * (1.0 / width) + EPS)
    gained = back * gain_two_ref[...]
    inner_sum = row_sum(mixed * gained) * (1.0 / width)
    grad_mixed[own_rows, :] = (
        inv_two * gained - mixed * (inv_two * inv_two * inv_two * inner_sum)
    ).astype(BF16)
    spread(4, row_piece(grad_mixed))
    out_ref[...] = hidden[...] * lax.dot_general(
        down_w[...], grad_mixed[...], NT, preferred_element_type=F32
    )


def shards(
    tokens, step_index, embed_table, gain_one, gate_weight, up_weight, down_weight, gain_two,
    query_weight, key_weight, value_weight, decay_weight, beta_weight, rate_log, decay_bias,
    beta_bias, cotangent,
):
    peers = lax.axis_size("inner")
    side = int(round(peers**0.5))
    chips = lax.axis_size("outer") // 2
    rows = tokens.shape[0]
    words, slab = embed_table.shape
    width = slab * peers
    hidden_dim = gate_weight.shape[1]
    key_dim, value_dim = query_weight.shape[1], value_weight.shape[1]
    share = rows // peers
    in_vmem = pl.BlockSpec(memory_space=pltpu.VMEM)
    in_smem = pl.BlockSpec(memory_space=pltpu.SMEM)
    in_place = pl.BlockSpec(memory_space=pl.ANY)
    vm = pltpu.VMEM
    messages = (side + 1) * (side - 1)
    state = (key_dim, value_dim)
    attribution = pl.pallas_call(
        functools.partial(kernel, chips),
        out_shape=jax.ShapeDtypeStruct((hidden_dim, rows), F32),
        in_specs=[in_smem] + [in_vmem] * 8 + [in_place] * 8,
        out_specs=in_vmem,
        scratch_shapes=[
            vm((words // 8, 8, slab), BF16),
            vm((hidden_dim, width), BF16),
            vm((hidden_dim, width), BF16),
            vm((hidden_dim, width), BF16),
            vm((width, 2 * key_dim + value_dim), BF16),
            vm((rows, value_dim), BF16),
            vm((8, width), F32),
            vm((peers, rows, slab), BF16),
            vm((rows, width), BF16),
            vm((hidden_dim, rows), F32),
            vm((2, side, side, share, width // 2), BF16),
            vm((2, side * (side - 1), share, width // 2), BF16),
            vm((2, side * (side - 1), share, width // 2), BF16),
            vm((2, side - 1, share, width // 2), BF16),
            vm((2, side - 1, share, width // 2), BF16),
            vm((2, side - 1, share, width // 2), BF16),
            vm((rows, width), BF16),
            vm((rows, width), BF16),
            vm((share, width), F32),
            vm((key_dim, key_dim), F32),
            vm((key_dim, key_dim), F32),
            vm(state, BF16),
            vm(state, BF16),
            vm(state, BF16),
            vm(state, BF16),
            vm(state, BF16),
            vm(state, BF16),
            pltpu.SemaphoreType.DMA((8,)),
            pltpu.SemaphoreType.DMA((5, 2, messages)),
            pltpu.SemaphoreType.DMA((5, 2, messages)),
            pltpu.SemaphoreType.DMA((4,)),
            pltpu.SemaphoreType.DMA((4,)),
        ],
        compiler_params=pltpu.CompilerParams(collective_id=0, has_side_effects=True),
        name="attribution",
    )(
        tokens,
        step_index.reshape(1, 1),
        rate_log.reshape(1, 1),
        decay_bias.reshape(1, 1),
        beta_bias.reshape(1, 1),
        gain_one.reshape(1, width),
        gain_two.reshape(1, width),
        decay_weight.reshape(1, width),
        beta_weight.reshape(1, width),
        embed_table.reshape(words // 8, 8, slab),
        gate_weight.T,
        up_weight.T,
        down_weight,
        query_weight,
        key_weight,
        value_weight,
        cotangent,
    )
    return attribution.T


def solution(mesh):
    placed = (
        P("outer"), P(), P(None, "inner"), P(), P(None, "inner"), P(None, "inner"),
        P("inner", None), P(), P(None, "inner"), P(None, "inner"), P(None, "inner"),
        P(None, "inner"), P(None, "inner"), P("inner"), P("inner"), P("inner"),
        P("outer", "inner"),
    )
    return jax.shard_map(
        shards, mesh=mesh, in_specs=placed, out_specs=P("outer", "inner"), check_vma=False
    )
```

```python
import functools

import jax
import jax.numpy as jnp
from jax import lax
from jax.experimental import pallas as pl
from jax.experimental.pallas import tpu as pltpu
from jax.sharding import PartitionSpec as P

STEPS = 32
EPS = 1e-06
F32 = jnp.float32
BF16 = jnp.bfloat16
MESH = pl.DeviceIdType.MESH
HIGHEST = lax.Precision.HIGHEST
NN = (((1,), (0,)), ((), ()))
NT = (((1,), (1,)), ((), ()))
TN = (((0,), (0,)), ((), ()))


def exact(left, right, dims=NN):
    return lax.dot_general(left, right, dims, precision=HIGHEST, preferred_element_type=F32)


def fast(left, right, dims=NN):
    return lax.dot_general(
        left.astype(BF16), right.astype(BF16), dims, preferred_element_type=F32
    )


def row_sum(values):
    return jnp.sum(values, axis=1, keepdims=True)


def split(value):
    high = value.astype(BF16)
    return high, (value - high.astype(F32)).astype(BF16)


def triple(left, right, dims=NN):
    left_high, left_low = split(left)
    right_high, right_low = split(right)

    def dot(one, two):
        return lax.dot_general(one, two, dims, preferred_element_type=F32)

    return dot(left_high, right_high) + (dot(left_high, right_low) + dot(left_low, right_high))


def times(left, right):
    high, low = split(left)
    return jnp.dot(high, right, preferred_element_type=F32) + jnp.dot(
        low, right, preferred_element_type=F32
    )


near = triple
solve = triple
gram = triple


def unit_inverse(lower, rows, cols):
    size = lower.shape[0]
    eye = (rows == cols).astype(F32)
    inverse, span = eye, 1
    while span < size:
        joined = (rows // (2 * span) == cols // (2 * span)) & (rows // span != cols // span)
        below = jnp.where(joined, lower, 0.0)
        if span == 1:
            inverse = eye - below
        else:
            inverse = inverse - solve(inverse, solve(below, inverse))
        span *= 2
    return inverse


def delta_prepare(query_pre, key_pre, values, decay_pre, beta_pre, cot, rate, decay_bias, beta_bias):
    size, key_dim = key_pre.shape
    query_inv = lax.rsqrt(row_sum(query_pre * query_pre) + EPS)
    key_inv = lax.rsqrt(row_sum(key_pre * key_pre) + EPS)
    queries = query_pre * (query_inv * key_dim ** (-0.5))
    keys = key_pre * key_inv
    shifted = decay_pre + decay_bias
    soft = jnp.maximum(shifted, 0.0) + jnp.log1p(jnp.exp(-jnp.abs(shifted)))
    log_decay = -jnp.exp(rate) * soft
    betas = 1.0 / (1.0 + jnp.exp(-(beta_pre + beta_bias)))

    rows = lax.broadcasted_iota(jnp.int32, (size, size), 0)
    cols = lax.broadcasted_iota(jnp.int32, (size, size), 1)
    lower = rows >= cols
    ones_lower = lower.astype(F32)
    cum_rows = exact(ones_lower, jnp.broadcast_to(log_decay, (size, size)))
    cum_cols = cum_rows.T
    ratio = jnp.where(lower, jnp.exp(jnp.where(lower, cum_rows - cum_cols, 0.0)), 0.0)
    cum = cum_rows[:, 0:1]
    cum_last = cum_cols[:, size - 1 : size]
    grown = jnp.exp(cum)
    left_over = jnp.exp(cum_last - cum)
    total = jnp.exp(cum_last[0:1, :])

    key_gram = gram(keys, keys, NT)
    ratio_gram = jnp.where(rows > cols, ratio * key_gram, 0.0)
    strict = betas * ratio_gram
    inverse = unit_inverse(strict, rows, cols)
    scores = ratio * near(queries, keys, NT)
    keys_grown = grown * keys
    queries_grown = grown * queries
    keys_tail = left_over * keys

    fresh_free = near(inverse, betas * values)
    fresh_map = near(inverse, betas * keys_grown)
    back_free = near(inverse, near(scores, cot, TN), TN)
    back_map = near(inverse, keys_tail, TN)
    eye = (
        lax.broadcasted_iota(jnp.int32, (key_dim, key_dim), 0)
        == lax.broadcasted_iota(jnp.int32, (key_dim, key_dim), 1)
    ).astype(F32)
    transition = total * eye - near(keys_tail, fresh_map, TN)
    transition_back = total * eye - near(fresh_map, keys_tail, TN)
    offset = near(keys_tail, fresh_free, TN)
    offset_back = near(queries_grown, cot, TN) - near(betas * keys_grown, back_free, TN)
    kept = dict(
        query_pre=query_pre, key_pre=key_pre, values=values, query_inv=query_inv, key_inv=key_inv,
        queries=queries, keys=keys, shifted=shifted, betas=betas, ratio=ratio, grown=grown,
        left_over=left_over, total=total, ratio_gram=ratio_gram, strict=strict, scores=scores,
        keys_grown=keys_grown, keys_tail=keys_tail, fresh_free=fresh_free, fresh_map=fresh_map,
        back_free=back_free, back_map=back_map, cot=cot, rate=rate,
    )
    return kept, (transition, offset), (transition_back, offset_back)


def delta_finish(kept, state, end_grad):
    k = kept
    size, key_dim = k["keys"].shape
    scale = key_dim ** (-0.5)
    rows = lax.broadcasted_iota(jnp.int32, (size, size), 0)
    cols = lax.broadcasted_iota(jnp.int32, (size, size), 1)
    fresh = k["fresh_free"] - near(k["fresh_map"], state)
    back = k["back_free"] + near(k["back_map"], end_grad)
    d_strict = jnp.where(rows > cols, -near(back, fresh, NT), 0.0)
    d_gram = d_strict * (k["betas"] * k["ratio"])
    d_scores = near(k["cot"], fresh, NT) * k["ratio"]
    residual = k["values"] - near(k["keys_grown"], state)
    d_values = k["betas"] * back
    d_betas = row_sum(back * residual) + row_sum(d_strict * k["ratio_gram"])
    cot_state = k["grown"] * near(k["cot"], state, NT)
    back_state = (k["grown"] * k["betas"]) * near(back, state, NT)
    fresh_end = k["left_over"] * near(fresh, end_grad, NT)
    d_queries = near(d_scores, k["keys"]) + cot_state
    d_keys_read = near(d_gram, k["keys"]) - back_state
    d_keys_write = near(d_gram, k["keys"], TN) + near(d_scores, k["queries"], TN) + fresh_end
    d_cum = row_sum(k["queries"] * d_queries) + row_sum(k["keys"] * (d_keys_read - d_keys_write))
    ends = jnp.sum(row_sum(k["keys"] * fresh_end), axis=0, keepdims=True) + k["total"] * jnp.sum(
        row_sum(state * end_grad), axis=0, keepdims=True
    )
    upper = (rows <= cols).astype(F32)
    d_log = exact(upper, jnp.broadcast_to(d_cum, (size, key_dim)))[:, 0:1] + ends

    query_inv, key_inv = k["query_inv"], k["key_inv"]
    d_query = (scale * query_inv) * (
        d_queries - k["query_pre"] * (query_inv * query_inv * row_sum(k["query_pre"] * d_queries))
    )
    d_keys = d_keys_read + d_keys_write
    d_key = key_inv * (d_keys - k["keys"] * row_sum(k["keys"] * d_keys))
    d_decay = d_log * (-jnp.exp(k["rate"])) * (1.0 / (1.0 + jnp.exp(-k["shifted"])))
    d_beta = d_betas * k["betas"] * (1.0 - k["betas"])
    return d_query, d_key, d_values, d_decay, d_beta


def ring_order(side):
    return sorted(range(1, side), key=lambda step: (-min(step, side - step), step))


def kernel(
    chips,
    tokens_ref, step_ref, rate_ref, decay_bias_ref, beta_bias_ref, gain_one_ref, gain_two_ref,
    decay_ref, beta_ref, table_hbm, gate_hbm, up_hbm, down_hbm, query_hbm, key_hbm, value_hbm,
    cot_hbm,
    out_ref,
    table, gate_w, up_w, down_w, main_w, cot_v, gates_w, emb, normed, hidden, part,
    heap_one, heap_two, sums, last_one, last_two,
    normed_two, grad_mixed, mixed_own, pair_map_out, pair_map_in, pair_off_out,
    pair_off_in, until_map, until_off, through_map, through_off, level_map_out, level_map_in,
    level_off_out, level_off_in, share_out, share_in,
    load_sem, send_sem, recv_sem, side_send, side_recv, level_send, level_recv,
):
    me = lax.axis_index("inner")
    outer = lax.axis_index("outer")
    peers = lax.axis_size("inner")
    side = int(round(peers**0.5))
    line, spot = me // side, lax.rem(me, side)
    chip, core = outer // 2, lax.rem(outer, 2)
    partner = {"outer": outer + 1 - 2 * core}
    turn = chip + core * (chips - 1 - 2 * chip)
    toward = 1 - 2 * core

    key_dim = query_hbm.shape[1]
    value_dim = value_hbm.shape[1]
    width = down_hbm.shape[1]
    half = width // 2
    rows = tokens_ref.shape[0]
    share = rows // peers
    slab = table.shape[2]

    loads = [
        pltpu.make_async_copy(gate_hbm, gate_w, load_sem.at[0]),
        pltpu.make_async_copy(up_hbm, up_w, load_sem.at[1]),
        pltpu.make_async_copy(down_hbm, down_w, load_sem.at[2]),
        pltpu.make_async_copy(query_hbm, main_w.at[:, pl.ds(0, key_dim)], load_sem.at[3]),
        pltpu.make_async_copy(key_hbm, main_w.at[:, pl.ds(key_dim, key_dim)], load_sem.at[4]),
        pltpu.make_async_copy(value_hbm, main_w.at[:, pl.ds(2 * key_dim, value_dim)], load_sem.at[5]),
        pltpu.make_async_copy(cot_hbm, cot_v, load_sem.at[6]),
    ]
    table_load = pltpu.make_async_copy(table_hbm, table, load_sem.at[7])
    table_load.start()

    barrier = pltpu.get_barrier_semaphore()
    for step in range(1, side):
        for peer in (
            lax.rem(line + step, side) * side + spot,
            line * side + lax.rem(spot + step, side),
        ):
            pl.semaphore_signal(barrier, inc=1, device_id={"inner": peer}, device_id_type=MESH)
    pl.semaphore_signal(barrier, inc=1, device_id=partner, device_id_type=MESH)
    for step in range(1, chips):
        device = {"outer": lax.rem(chip + step, chips) * 2 + core}
        pl.semaphore_signal(barrier, inc=1, device_id=device, device_id_type=MESH)
    for load in loads:
        load.start()

    row_id = lax.broadcasted_iota(jnp.int32, (8, width), 0)
    gates_w[...] = jnp.where(
        row_id == 0,
        decay_ref[...].astype(F32),
        jnp.where(row_id == 1, beta_ref[...].astype(F32), 0.0),
    )

    table_load.wait()
    tile_row = lax.broadcasted_iota(jnp.int32, (8, slab), 0)

    def pick(index, carry):
        found = []
        for part_of in range(2):
            tile = jnp.zeros((8, slab), F32)
            for row in range(8):
                token = tokens_ref[index * 16 + part_of * 8 + row]
                near_rows = table[lax.shift_right_logical(token, 3)].astype(F32)
                chosen = jnp.sum(
                    jnp.where(tile_row == (token & 7), near_rows, 0.0), axis=0, keepdims=True
                )
                tile = jnp.where(tile_row == row, chosen, tile)
            found.append(tile)
        emb[me, pl.ds(pl.multiple_of(index * 16, 16), 16), :] = jnp.concatenate(
            found, axis=0
        ).astype(BF16)
        return carry

    lax.fori_loop(0, rows // 16, pick, 0)
    pl.semaphore_wait(barrier, 2 * (side - 1) + chips)

    def to_axis(across, step):
        if across:
            return line * side + lax.rem(spot + step, side)
        return lax.rem(line + step, side) * side + spot

    def send(stage, way, index, source, target, peer):
        copy = pltpu.make_async_remote_copy(
            src_ref=source,
            dst_ref=target,
            send_sem=send_sem.at[stage, way, index],
            recv_sem=recv_sem.at[stage, way, index],
            device_id={"inner": peer},
            device_id_type=MESH,
        )
        copy.start()
        return copy

    order = ring_order(side)

    def spread(stage, piece):
        first_hop, second_hop = [{}, {}], []
        for step in order:
            for way in range(2):
                own = piece(me, way)
                first_hop[way][step] = send(stage, way, step - 1, own, own, to_axis(way, step))
        for step in order:
            for way in range(2):
                own = piece(me, way)
                second_hop.append(
                    send(stage, way, side - 1 + step - 1, own, own, to_axis(1 - way, step))
                )
        for gone in reversed(order):
            for way in range(2):
                first_hop[way][gone].wait_recv()
                got = piece(to_axis(way, side - gone), way)
                for step in order:
                    index = (side - 1) * (1 + gone) + step - 1
                    second_hop.append(send(stage, way, index, got, got, to_axis(1 - way, step)))
        for copy in second_hop:
            copy.wait()
        for way in range(2):
            for step in order:
                first_hop[way][step].wait_send()

    def reduce_send(stage, heap, way):
        hops = {}
        for apart in order + [0]:
            for step in order:
                if way == 0:
                    at = (lax.rem(line + apart, side), lax.rem(spot + step, side))
                else:
                    at = (lax.rem(line + step, side), lax.rem(spot + apart, side))
                index = apart * (side - 1) + step - 1
                hops[apart, step] = send(
                    stage, way, index, part.at[way, at[0], at[1]], heap.at[way, index],
                    to_axis(1 - way, step),
                )
        return hops

    def reduce_finish(stage, heap, last, hops):
        own, second_hop = [None, None], [[], []]
        for apart in order + [0]:
            for way in range(2):
                if way == 0:
                    at = (lax.rem(line + apart, side), spot)
                else:
                    at = (line, lax.rem(spot + apart, side))
                total = part[way, at[0], at[1]].astype(F32)
                for step in reversed(order):
                    hops[way][apart, step].wait_recv()
                    total = total + heap[way, apart * (side - 1) + step - 1].astype(F32)
                if apart == 0:
                    own[way] = total
                else:
                    sums[way, apart - 1] = total.astype(BF16)
                    second_hop[way].append(
                        (apart, send(
                            stage, way, side * (side - 1) + apart - 1, sums.at[way, apart - 1],
                            last.at[way, apart - 1], to_axis(way, apart),
                        ))
                    )
        for way in range(2):
            for apart, copy in second_hop[way]:
                copy.wait()
                own[way] = own[way] + last[way, apart - 1].astype(F32)
            for copy in hops[way].values():
                copy.wait_send()
        return jnp.concatenate(own, axis=1)

    spread(0, lambda owner, way: emb.at[owner, pl.ds(way * (rows // 2), rows // 2), :])

    def norm_one(index, carry):
        at = pl.ds(pl.multiple_of(index * 16, 16), 16)
        values = [emb[owner, at, :].astype(F32) for owner in range(peers)]
        squares = values[0] * values[0]
        for value in values[1:]:
            squares = squares + value * value
        scale = lax.rsqrt(row_sum(squares) * (1.0 / width) + EPS)
        for owner, value in enumerate(values):
            cut = slice(owner * slab, (owner + 1) * slab)
            normed[at, cut] = (value * scale * gain_one_ref[:, cut]).astype(BF16)
        return carry

    lax.fori_loop(0, rows // 16, norm_one, 0, unroll=2)
    loads[0].wait()
    loads[1].wait()
    gate_rows = lax.dot_general(normed[...], gate_w[...], NT, preferred_element_type=F32)
    up_rows = lax.dot_general(normed[...], up_w[...], NT, preferred_element_type=F32)
    active = gate_rows * (1.0 / (1.0 + jnp.exp(-gate_rows))) * up_rows
    path_scale = (step_ref[...].astype(F32) + 0.5) / STEPS
    scaled = (path_scale * active).astype(BF16)
    loads[2].wait()

    def partial_half(way, product):
        for first in range(way * half, way * half + half, 256):
            block = product(slice(first, first + 256)).astype(BF16)
            at = slice(first - way * half, first - way * half + 256)
            part[way, :, :, :, at] = block.reshape(side, side, share, 256)

    hops = []
    for way in range(2):
        partial_half(
            way, lambda at: jnp.dot(scaled, down_w[:, at], preferred_element_type=F32)
        )
        hops.append(reduce_send(1, heap_one, way))
    hidden[...] = active.T
    own_rows = pl.ds(pl.multiple_of(me * share, share), share)
    own_emb = jnp.concatenate([emb[owner, own_rows, :] for owner in range(peers)], axis=1)
    mixed = own_emb.astype(F32) + reduce_finish(1, heap_one, last_one, hops)
    mixed_own[...] = mixed
    inv_two = lax.rsqrt(row_sum(mixed * mixed) * (1.0 / width) + EPS)
    normed_two[own_rows, :] = (mixed * inv_two * gain_two_ref[...]).astype(BF16)

    def row_piece(array):
        return lambda owner, way: array.at[
            pl.ds(pl.multiple_of(owner * share, share), share), pl.ds(way * half, half)
        ]

    spread(2, row_piece(normed_two))
    for load in loads[3:]:
        load.wait()
    main = jnp.dot(normed_two[...], main_w[...], preferred_element_type=F32)
    gates = lax.dot_general(
        normed_two[...], gates_w[...].astype(BF16), NT, preferred_element_type=F32
    )
    kept, ahead_map, back_map = delta_prepare(
        main[:, :key_dim],
        main[:, key_dim : 2 * key_dim],
        main[:, 2 * key_dim :],
        gates[:, 0:1],
        gates[:, 1:2],
        cot_v[...].astype(F32),
        rate_ref[...],
        decay_bias_ref[...],
        beta_bias_ref[...],
    )

    first = core == 0
    own_map = jnp.where(first, ahead_map[0], back_map[0])
    own_off = jnp.where(first, ahead_map[1], back_map[1])
    pair_map_out[...] = jnp.where(first, back_map[0], ahead_map[0])
    pair_off_out[...] = jnp.where(first, back_map[1], ahead_map[1]).astype(BF16)

    def to_side(index, source, target, device):
        return pltpu.make_async_remote_copy(
            src_ref=source,
            dst_ref=target,
            send_sem=side_send.at[index],
            recv_sem=side_recv.at[index],
            device_id=device,
            device_id_type=MESH,
        )

    pair_copies = [
        to_side(0, pair_map_out, pair_map_in, partner),
        to_side(1, pair_off_out, pair_off_in, partner),
    ]
    for copy in pair_copies:
        copy.start()
    for copy in pair_copies:
        copy.wait()
    through_map[...] = triple(pair_map_in[...], own_map)
    through_off[...] = triple(pair_map_in[...], own_off) + pair_off_in[...].astype(F32)
    until_map[...] = (
        lax.broadcasted_iota(jnp.int32, until_map.shape, 0)
        == lax.broadcasted_iota(jnp.int32, until_map.shape, 1)
    ).astype(F32)
    until_off[...] = jnp.zeros_like(until_off)

    levels = chips.bit_length() - 1

    def level_copy(kind, level, step):
        out, into = ((level_off_out, level_off_in), (level_map_out, level_map_in))[kind]
        return pltpu.make_async_remote_copy(
            src_ref=out.at[level],
            dst_ref=into.at[level],
            send_sem=level_send.at[kind, 2**level - 1 + step - 1],
            recv_sem=level_recv.at[kind, level],
            device_id={"outer": lax.rem(chip + toward * step + chips, chips) * 2 + core},
            device_id_type=MESH,
        )

    for level in range(levels):
        span = 2 ** level
        final = level == levels - 1
        place = lax.rem(turn, 2 * span)
        leading = turn < 2 * span

        @pl.when(place == span - 1)
        def _():
            level_off_out[level] = through_off[...].astype(BF16)
            if not final:
                level_map_out[level] = through_map[...].astype(BF16)
            for step in range(span, 0, -1):
                if not final:
                    @pl.when(jnp.logical_not(leading))
                    def _():
                        level_copy(1, level, step).start()
                level_copy(0, level, step).start()

        @pl.when(place >= span)
        def _():
            if not final:
                @pl.when(jnp.logical_not(leading))
                def _():
                    level_copy(1, level, 1).wait_recv()
            level_copy(0, level, 1).wait_recv()
            got = level_off_in[level]
            until_off[...] = until_off[...] + times(until_map[...], got)
            if not final:
                @pl.when(place == 2 * span - 1)
                def _():
                    through_off[...] = through_off[...] + times(through_map[...], got)

                @pl.when(jnp.logical_not(leading))
                def _():
                    got_map = level_map_in[level]
                    until_map[...] = times(until_map[...], got_map)
                    through_map[...] = times(through_map[...], got_map)

    carried = until_off[...]
    share_out[...] = (triple(own_map, carried) + own_off).astype(BF16)
    swap = to_side(2, share_out, share_in, partner)
    swap.start()
    swap.wait()
    other = share_in[...].astype(F32)
    state = jnp.where(first, carried, other)
    end_grad = jnp.where(first, other, carried)
    d_query, d_key, d_value, d_decay, d_beta = delta_finish(kept, state, end_grad)

    for level in range(levels):
        span = 2 ** level

        @pl.when(lax.rem(turn, 2 * span) == span - 1)
        def _():
            for step in range(span, 0, -1):
                level_copy(0, level, step).wait_send()
                if level < levels - 1:
                    @pl.when(jnp.logical_not(turn < 2 * span))
                    def _():
                        level_copy(1, level, step).wait_send()

    grads = jnp.concatenate([d_query, d_key, d_value], axis=1).astype(BF16)
    d_decay = d_decay.astype(BF16).astype(F32)
    d_beta = d_beta.astype(BF16).astype(F32)

    def back_block(at):
        block = lax.dot_general(grads, main_w[at, :], NT, preferred_element_type=F32)
        return block + d_decay * gates_w[0:1, at] + d_beta * gates_w[1:2, at]

    hops = []
    for way in range(2):
        partial_half(way, back_block)
        hops.append(reduce_send(3, heap_two, way))
    back = reduce_finish(3, heap_two, last_two, hops)
    mixed = mixed_own[...]
    inv_two = lax.rsqrt(row_sum(mixed * mixed) * (1.0 / width) + EPS)
    gained = back * gain_two_ref[...]
    inner_sum = row_sum(mixed * gained) * (1.0 / width)
    grad_mixed[own_rows, :] = (
        inv_two * gained - mixed * (inv_two * inv_two * inv_two * inner_sum)
    ).astype(BF16)
    spread(4, row_piece(grad_mixed))
    out_ref[...] = hidden[...] * lax.dot_general(
        down_w[...], grad_mixed[...], NT, preferred_element_type=F32
    )


def shards(
    tokens, step_index, embed_table, gain_one, gate_weight, up_weight, down_weight, gain_two,
    query_weight, key_weight, value_weight, decay_weight, beta_weight, rate_log, decay_bias,
    beta_bias, cotangent,
):
    peers = lax.axis_size("inner")
    side = int(round(peers**0.5))
    chips = lax.axis_size("outer") // 2
    rows = tokens.shape[0]
    words, slab = embed_table.shape
    width = slab * peers
    hidden_dim = gate_weight.shape[1]
    key_dim, value_dim = query_weight.shape[1], value_weight.shape[1]
    share = rows // peers
    in_vmem = pl.BlockSpec(memory_space=pltpu.VMEM)
    in_smem = pl.BlockSpec(memory_space=pltpu.SMEM)
    in_place = pl.BlockSpec(memory_space=pl.ANY)
    vm = pltpu.VMEM
    messages = (side + 1) * (side - 1)
    levels = chips.bit_length() - 1
    state = (key_dim, value_dim)
    attribution = pl.pallas_call(
        functools.partial(kernel, chips),
        out_shape=jax.ShapeDtypeStruct((hidden_dim, rows), F32),
        in_specs=[in_smem] + [in_vmem] * 8 + [in_place] * 8,
        out_specs=in_vmem,
        scratch_shapes=[
            vm((words // 8, 8, slab), BF16),
            vm((hidden_dim, width), BF16),
            vm((hidden_dim, width), BF16),
            vm((hidden_dim, width), BF16),
            vm((width, 2 * key_dim + value_dim), BF16),
            vm((rows, value_dim), BF16),
            vm((8, width), F32),
            vm((peers, rows, slab), BF16),
            vm((rows, width), BF16),
            vm((hidden_dim, rows), F32),
            vm((2, side, side, share, width // 2), BF16),
            vm((2, side * (side - 1), share, width // 2), BF16),
            vm((2, side * (side - 1), share, width // 2), BF16),
            vm((2, side - 1, share, width // 2), BF16),
            vm((2, side - 1, share, width // 2), BF16),
            vm((2, side - 1, share, width // 2), BF16),
            vm((rows, width), BF16),
            vm((rows, width), BF16),
            vm((share, width), F32),
            vm((key_dim, key_dim), F32),
            vm((key_dim, key_dim), F32),
            vm(state, BF16),
            vm(state, BF16),
            vm((key_dim, key_dim), F32),
            vm(state, F32),
            vm((key_dim, key_dim), F32),
            vm(state, F32),
            vm((levels, key_dim, key_dim), BF16),
            vm((levels, key_dim, key_dim), BF16),
            vm((levels,) + state, BF16),
            vm((levels,) + state, BF16),
            vm(state, BF16),
            vm(state, BF16),
            pltpu.SemaphoreType.DMA((8,)),
            pltpu.SemaphoreType.DMA((5, 2, messages)),
            pltpu.SemaphoreType.DMA((5, 2, messages)),
            pltpu.SemaphoreType.DMA((3,)),
            pltpu.SemaphoreType.DMA((3,)),
            pltpu.SemaphoreType.DMA((2, chips - 1)),
            pltpu.SemaphoreType.DMA((2, levels)),
        ],
        compiler_params=pltpu.CompilerParams(collective_id=0, has_side_effects=True),
        name="attribution",
    )(
        tokens,
        step_index.reshape(1, 1),
        rate_log.reshape(1, 1),
        decay_bias.reshape(1, 1),
        beta_bias.reshape(1, 1),
        gain_one.reshape(1, width),
        gain_two.reshape(1, width),
        decay_weight.reshape(1, width),
        beta_weight.reshape(1, width),
        embed_table.reshape(words // 8, 8, slab),
        gate_weight.T,
        up_weight.T,
        down_weight,
        query_weight,
        key_weight,
        value_weight,
        cotangent,
    )
    return attribution.T


def solution(mesh):
    placed = (
        P("outer"), P(), P(None, "inner"), P(), P(None, "inner"), P(None, "inner"),
        P("inner", None), P(), P(None, "inner"), P(None, "inner"), P(None, "inner"),
        P(None, "inner"), P(None, "inner"), P("inner"), P("inner"), P("inner"),
        P("outer", "inner"),
    )
    return jax.shard_map(
        shards, mesh=mesh, in_specs=placed, out_specs=P("outer", "inner"), check_vma=False
    )
```

```python
import functools

import jax
import jax.numpy as jnp
from jax import lax
from jax.experimental import pallas as pl
from jax.experimental.pallas import tpu as pltpu
from jax.sharding import PartitionSpec as P

STEPS = 32
EPS = 1e-06
F32 = jnp.float32
BF16 = jnp.bfloat16
MESH = pl.DeviceIdType.MESH
HIGHEST = lax.Precision.HIGHEST
NN = (((1,), (0,)), ((), ()))
NT = (((1,), (1,)), ((), ()))
TN = (((0,), (0,)), ((), ()))


def exact(left, right, dims=NN):
    return lax.dot_general(left, right, dims, precision=HIGHEST, preferred_element_type=F32)


def fast(left, right, dims=NN):
    return lax.dot_general(
        left.astype(BF16), right.astype(BF16), dims, preferred_element_type=F32
    )


def row_sum(values):
    return jnp.sum(values, axis=1, keepdims=True)


def split(value):
    high = value.astype(BF16)
    return high, (value - high.astype(F32)).astype(BF16)


def triple(left, right, dims=NN):
    left_high, left_low = split(left)
    right_high, right_low = split(right)

    def dot(one, two):
        return lax.dot_general(one, two, dims, preferred_element_type=F32)

    return dot(left_high, right_high) + (dot(left_high, right_low) + dot(left_low, right_high))


def times(left, right):
    high, low = split(left)
    return jnp.dot(high, right, preferred_element_type=F32) + jnp.dot(
        low, right, preferred_element_type=F32
    )


def running(ones, column):
    wide = jnp.broadcast_to(column, (column.shape[0], 128))
    high, rest = wide.astype(BF16), wide
    total = None
    for _ in range(3):
        high = rest.astype(BF16)
        rest = rest - high.astype(F32)
        term = jnp.dot(ones, high, preferred_element_type=F32)
        total = term if total is None else total + term
    return total


near = fast
solve = triple
gram = triple


def unit_inverse(lower):
    size = lower.shape[0]
    if size > 128:
        middle = size // 2
        upper_left = unit_inverse(lower[:middle, :middle])
        lower_right = unit_inverse(lower[middle:, middle:])
        below = -solve(lower_right, solve(lower[middle:, :middle], upper_left))
        top = jnp.concatenate([upper_left, jnp.zeros_like(below)], axis=1)
        return jnp.concatenate([top, jnp.concatenate([below, lower_right], axis=1)], axis=0)
    apart = lax.broadcasted_iota(jnp.int32, (size, size), 0) ^ lax.broadcasted_iota(
        jnp.int32, (size, size), 1
    )
    inverse = jnp.where(apart == 0, 1.0, 0.0) - jnp.where(apart == 1, lower, 0.0)
    for level in range(1, size.bit_length() - 1):
        joined = jnp.where(lax.shift_right_logical(apart, level) == 1, lower, 0.0)
        inverse = inverse - solve(inverse, solve(joined, inverse))
    return inverse


def delta_prepare(query_pre, key_pre, values, decay_pre, beta_pre, cot, rate, decay_bias, beta_bias):
    size, key_dim = key_pre.shape
    query_inv = lax.rsqrt(row_sum(query_pre * query_pre) + EPS)
    key_inv = lax.rsqrt(row_sum(key_pre * key_pre) + EPS)
    queries = query_pre * (query_inv * key_dim ** (-0.5))
    keys = key_pre * key_inv
    shifted = decay_pre + decay_bias
    soft = jnp.maximum(shifted, 0.0) + jnp.log1p(jnp.exp(-jnp.abs(shifted)))
    log_decay = -jnp.exp(rate) * soft
    betas = 1.0 / (1.0 + jnp.exp(-(beta_pre + beta_bias)))

    rows = lax.broadcasted_iota(jnp.int32, (size, size), 0)
    cols = lax.broadcasted_iota(jnp.int32, (size, size), 1)
    lower = rows >= cols
    cum_wide = running(lower.astype(F32).astype(BF16), log_decay)
    cum_rows = jnp.concatenate([cum_wide] * (size // 128), axis=1)
    cum_cols = jnp.concatenate([cum_wide.T] * (size // 128), axis=0)
    ratio = jnp.where(lower, jnp.exp(jnp.where(lower, cum_rows - cum_cols, 0.0)), 0.0)
    cum = cum_rows[:, 0:1]
    cum_last = cum_cols[:, size - 1 : size]
    grown = jnp.exp(cum)
    left_over = jnp.exp(cum_last - cum)
    total = jnp.exp(cum_last[0:1, :])

    key_gram = gram(keys, keys, NT)
    ratio_gram = jnp.where(rows > cols, ratio * key_gram, 0.0)
    strict = betas * ratio_gram
    inverse = unit_inverse(strict)
    scores = ratio * near(queries, keys, NT)
    keys_grown = grown * keys
    queries_grown = grown * queries
    keys_tail = left_over * keys

    fresh_free = near(inverse, betas * values)
    fresh_map = near(inverse, betas * keys_grown)
    back_free = near(inverse, near(scores, cot, TN), TN)
    back_map = near(inverse, keys_tail, TN)
    eye = (
        lax.broadcasted_iota(jnp.int32, (key_dim, key_dim), 0)
        == lax.broadcasted_iota(jnp.int32, (key_dim, key_dim), 1)
    ).astype(F32)
    transition = total * eye - near(keys_tail, fresh_map, TN)
    transition_back = total * eye - near(fresh_map, keys_tail, TN)
    offset = near(keys_tail, fresh_free, TN)
    offset_back = near(queries_grown, cot, TN) - near(betas * keys_grown, back_free, TN)
    kept = dict(
        query_pre=query_pre, key_pre=key_pre, values=values, query_inv=query_inv, key_inv=key_inv,
        queries=queries, keys=keys, shifted=shifted, betas=betas, ratio=ratio, grown=grown,
        left_over=left_over, total=total, ratio_gram=ratio_gram, strict=strict, scores=scores,
        keys_grown=keys_grown, keys_tail=keys_tail, fresh_free=fresh_free, fresh_map=fresh_map,
        back_free=back_free, back_map=back_map, cot=cot, rate=rate,
    )
    return kept, (transition, offset), (transition_back, offset_back)


def delta_finish(kept, state, end_grad):
    k = kept
    size, key_dim = k["keys"].shape
    scale = key_dim ** (-0.5)
    rows = lax.broadcasted_iota(jnp.int32, (size, size), 0)
    cols = lax.broadcasted_iota(jnp.int32, (size, size), 1)
    fresh = k["fresh_free"] - near(k["fresh_map"], state)
    back = k["back_free"] + near(k["back_map"], end_grad)
    d_strict = jnp.where(rows > cols, -near(back, fresh, NT), 0.0)
    d_gram = d_strict * (k["betas"] * k["ratio"])
    d_scores = near(k["cot"], fresh, NT) * k["ratio"]
    residual = k["values"] - near(k["keys_grown"], state)
    d_values = k["betas"] * back
    d_betas = row_sum(back * residual) + row_sum(d_strict * k["ratio_gram"])
    cot_state = k["grown"] * near(k["cot"], state, NT)
    back_state = (k["grown"] * k["betas"]) * near(back, state, NT)
    fresh_end = k["left_over"] * near(fresh, end_grad, NT)
    d_queries = near(d_scores, k["keys"]) + cot_state
    d_keys_read = near(d_gram, k["keys"]) - back_state
    d_keys_write = near(d_gram, k["keys"], TN) + near(d_scores, k["queries"], TN) + fresh_end
    d_cum = row_sum(k["queries"] * d_queries) + row_sum(k["keys"] * (d_keys_read - d_keys_write))
    ends = jnp.sum(row_sum(k["keys"] * fresh_end), axis=0, keepdims=True) + k["total"] * jnp.sum(
        row_sum(state * end_grad), axis=0, keepdims=True
    )
    upper = (rows <= cols).astype(F32).astype(BF16)
    d_log = running(upper, d_cum)[:, 0:1] + ends

    query_inv, key_inv = k["query_inv"], k["key_inv"]
    d_query = (scale * query_inv) * (
        d_queries - k["query_pre"] * (query_inv * query_inv * row_sum(k["query_pre"] * d_queries))
    )
    d_keys = d_keys_read + d_keys_write
    d_key = key_inv * (d_keys - k["keys"] * row_sum(k["keys"] * d_keys))
    d_decay = d_log * (-jnp.exp(k["rate"])) * (1.0 / (1.0 + jnp.exp(-k["shifted"])))
    d_beta = d_betas * k["betas"] * (1.0 - k["betas"])
    return d_query, d_key, d_values, d_decay, d_beta


def ring_order(side):
    return sorted(range(1, side), key=lambda step: (-min(step, side - step), step))


def kernel(
    chips,
    tokens_hbm, step_ref, rate_ref, decay_bias_ref, beta_bias_ref, gain_one_hbm, gain_two_hbm,
    decay_hbm, beta_hbm, table_hbm, gate_hbm, up_hbm, down_hbm, query_hbm, key_hbm, value_hbm,
    cot_hbm,
    out_ref,
    tokens_ref, gain_one_ref, gain_two_ref, decay_ref, beta_ref, table, gate_w, up_w, down_w, main_w, cot_v, gates_w, emb, normed, hidden, part,
    heap_one, heap_two, sums, last_one, last_two,
    normed_two, grad_mixed, mixed_own, pair_map_out, pair_map_in, pair_off_out,
    pair_off_in, until_map, until_off, share_map, share_off, through_map, through_off, level_map_out, level_map_in,
    level_off_out, level_off_in, share_out, share_in,
    small_sem, load_sem, send_sem, recv_sem, side_send, side_recv, level_send, level_recv,
):
    me = lax.axis_index("inner")
    outer = lax.axis_index("outer")
    peers = lax.axis_size("inner")
    side = int(round(peers**0.5))
    line, spot = me // side, lax.rem(me, side)
    chip, core = outer // 2, lax.rem(outer, 2)
    partner = {"outer": outer + 1 - 2 * core}
    turn = chip + core * (chips - 1 - 2 * chip)
    toward = 1 - 2 * core

    key_dim = query_hbm.shape[1]
    value_dim = value_hbm.shape[1]
    width = down_hbm.shape[1]
    half = width // 2
    rows = tokens_ref.shape[0]
    share = rows // peers
    slab = table.shape[2]

    barrier = pltpu.get_barrier_semaphore()
    for step in range(1, side):
        for peer in (
            lax.rem(line + step, side) * side + spot,
            line * side + lax.rem(spot + step, side),
        ):
            pl.semaphore_signal(barrier, inc=1, device_id={"inner": peer}, device_id_type=MESH)
    pl.semaphore_signal(barrier, inc=1, device_id=partner, device_id_type=MESH)
    for step in range(1, chips):
        device = {"outer": lax.rem(chip + step, chips) * 2 + core}
        pl.semaphore_signal(barrier, inc=1, device_id=device, device_id_type=MESH)

    small = [
        pltpu.make_async_copy(source, target, small_sem.at[index])
        for index, (source, target) in enumerate((
            (tokens_hbm, tokens_ref), (gain_one_hbm, gain_one_ref), (gain_two_hbm, gain_two_ref),
            (decay_hbm, decay_ref), (beta_hbm, beta_ref),
        ))
    ]
    small[0].start()
    loads = [
        pltpu.make_async_copy(gate_hbm, gate_w, load_sem.at[0]),
        pltpu.make_async_copy(up_hbm, up_w, load_sem.at[1]),
        pltpu.make_async_copy(down_hbm, down_w, load_sem.at[2]),
        pltpu.make_async_copy(query_hbm, main_w.at[:, pl.ds(0, key_dim)], load_sem.at[3]),
        pltpu.make_async_copy(key_hbm, main_w.at[:, pl.ds(key_dim, key_dim)], load_sem.at[4]),
        pltpu.make_async_copy(value_hbm, main_w.at[:, pl.ds(2 * key_dim, value_dim)], load_sem.at[5]),
        pltpu.make_async_copy(cot_hbm, cot_v, load_sem.at[6]),
    ]
    table_load = pltpu.make_async_copy(table_hbm, table, load_sem.at[7])
    table_load.start()
    for load in small[1:]:
        load.start()
    for load in loads:
        load.start()

    for load in small:
        load.wait()
    row_id = lax.broadcasted_iota(jnp.int32, (8, width), 0)
    gates_w[...] = jnp.where(
        row_id == 0,
        decay_ref[...].astype(F32),
        jnp.where(row_id == 1, beta_ref[...].astype(F32), 0.0),
    )

    table_load.wait()
    tile_row = lax.broadcasted_iota(jnp.int32, (8, slab), 0)

    def pick(index, carry):
        found = []
        for part_of in range(2):
            tile = jnp.zeros((8, slab), F32)
            for row in range(8):
                token = tokens_ref[index * 16 + part_of * 8 + row]
                near_rows = table[lax.shift_right_logical(token, 3)].astype(F32)
                chosen = jnp.sum(
                    jnp.where(tile_row == (token & 7), near_rows, 0.0), axis=0, keepdims=True
                )
                tile = jnp.where(tile_row == row, chosen, tile)
            found.append(tile)
        emb[me, pl.ds(pl.multiple_of(index * 16, 16), 16), :] = jnp.concatenate(
            found, axis=0
        ).astype(BF16)
        return carry

    lax.fori_loop(0, rows // 16, pick, 0)
    pl.semaphore_wait(barrier, 2 * (side - 1) + chips)

    def to_axis(across, step):
        if across:
            return line * side + lax.rem(spot + step, side)
        return lax.rem(line + step, side) * side + spot

    def send(stage, way, index, source, target, peer):
        copy = pltpu.make_async_remote_copy(
            src_ref=source,
            dst_ref=target,
            send_sem=send_sem.at[stage, way, index],
            recv_sem=recv_sem.at[stage, way, index],
            device_id={"inner": peer},
            device_id_type=MESH,
        )
        copy.start()
        return copy

    order = ring_order(side)

    def spread(stage, piece):
        first_hop, second_hop = [{}, {}], []
        for step in order:
            for way in range(2):
                own = piece(me, way)
                first_hop[way][step] = send(stage, way, step - 1, own, own, to_axis(way, step))
        for step in order:
            for way in range(2):
                own = piece(me, way)
                second_hop.append(
                    send(stage, way, side - 1 + step - 1, own, own, to_axis(1 - way, step))
                )
        for gone in reversed(order):
            for way in range(2):
                first_hop[way][gone].wait_recv()
                got = piece(to_axis(way, side - gone), way)
                for step in order:
                    index = (side - 1) * (1 + gone) + step - 1
                    second_hop.append(send(stage, way, index, got, got, to_axis(1 - way, step)))
        for copy in second_hop:
            copy.wait()
        for way in range(2):
            for step in order:
                first_hop[way][step].wait_send()

    def reduce_send(stage, heap, way):
        hops = {}
        for apart in order + [0]:
            for step in order:
                if way == 0:
                    at = (lax.rem(line + apart, side), lax.rem(spot + step, side))
                else:
                    at = (lax.rem(line + step, side), lax.rem(spot + apart, side))
                index = apart * (side - 1) + step - 1
                hops[apart, step] = send(
                    stage, way, index, part.at[way, at[0], at[1]], heap.at[way, index],
                    to_axis(1 - way, step),
                )
        return hops

    def reduce_finish(stage, heap, last, hops):
        own, second_hop = [None, None], [[], []]
        for apart in order + [0]:
            for way in range(2):
                if way == 0:
                    at = (lax.rem(line + apart, side), spot)
                else:
                    at = (line, lax.rem(spot + apart, side))
                total = part[way, at[0], at[1]].astype(F32)
                for step in reversed(order):
                    hops[way][apart, step].wait_recv()
                    total = total + heap[way, apart * (side - 1) + step - 1].astype(F32)
                if apart == 0:
                    own[way] = total
                else:
                    sums[way, apart - 1] = total.astype(BF16)
                    second_hop[way].append(
                        (apart, send(
                            stage, way, side * (side - 1) + apart - 1, sums.at[way, apart - 1],
                            last.at[way, apart - 1], to_axis(way, apart),
                        ))
                    )
        for way in range(2):
            for apart, copy in second_hop[way]:
                copy.wait()
                own[way] = own[way] + last[way, apart - 1].astype(F32)
            for copy in hops[way].values():
                copy.wait_send()
        return jnp.concatenate(own, axis=1)

    spread(0, lambda owner, way: emb.at[owner, pl.ds(way * (rows // 2), rows // 2), :])

    def norm_one(index, carry):
        at = pl.ds(pl.multiple_of(index * 16, 16), 16)
        values = [emb[owner, at, :].astype(F32) for owner in range(peers)]
        squares = values[0] * values[0]
        for value in values[1:]:
            squares = squares + value * value
        scale = lax.rsqrt(row_sum(squares) * (1.0 / width) + EPS)
        for owner, value in enumerate(values):
            cut = slice(owner * slab, (owner + 1) * slab)
            normed[at, cut] = (value * scale * gain_one_ref[:, cut]).astype(BF16)
        return carry

    lax.fori_loop(0, rows // 16, norm_one, 0, unroll=2)
    loads[0].wait()
    loads[1].wait()
    gate_rows = lax.dot_general(normed[...], gate_w[...], NT, preferred_element_type=F32)
    up_rows = lax.dot_general(normed[...], up_w[...], NT, preferred_element_type=F32)
    active = gate_rows * (1.0 / (1.0 + jnp.exp(-gate_rows))) * up_rows
    path_scale = (step_ref[0].astype(F32) + 0.5) / STEPS
    scaled = (path_scale * active).astype(BF16)
    loads[2].wait()

    def partial_half(way, product):
        for first in range(way * half, way * half + half, 256):
            block = product(slice(first, first + 256)).astype(BF16)
            at = slice(first - way * half, first - way * half + 256)
            part[way, :, :, :, at] = block.reshape(side, side, share, 256)

    hops = []
    for way in range(2):
        partial_half(
            way, lambda at: jnp.dot(scaled, down_w[:, at], preferred_element_type=F32)
        )
        hops.append(reduce_send(1, heap_one, way))
    hidden[...] = active.T
    own_rows = pl.ds(pl.multiple_of(me * share, share), share)
    own_emb = jnp.concatenate([emb[owner, own_rows, :] for owner in range(peers)], axis=1)
    mixed = own_emb.astype(F32) + reduce_finish(1, heap_one, last_one, hops)
    mixed_own[...] = mixed
    inv_two = lax.rsqrt(row_sum(mixed * mixed) * (1.0 / width) + EPS)
    normed_two[own_rows, :] = (mixed * inv_two * gain_two_ref[...]).astype(BF16)

    def row_piece(array):
        return lambda owner, way: array.at[
            pl.ds(pl.multiple_of(owner * share, share), share), pl.ds(way * half, half)
        ]

    spread(2, row_piece(normed_two))
    for load in loads[3:]:
        load.wait()
    main = jnp.dot(normed_two[...], main_w[...], preferred_element_type=F32)
    gates = lax.dot_general(
        normed_two[...], gates_w[...].astype(BF16), NT, preferred_element_type=F32
    )
    kept, ahead_map, back_map = delta_prepare(
        main[:, :key_dim],
        main[:, key_dim : 2 * key_dim],
        main[:, 2 * key_dim :],
        gates[:, 0:1],
        gates[:, 1:2],
        cot_v[...].astype(F32),
        jnp.full((1, 1), rate_ref[0]),
        decay_bias_ref[0],
        beta_bias_ref[0],
    )

    first = core == 0
    own_map = jnp.where(first, ahead_map[0], back_map[0])
    own_off = jnp.where(first, ahead_map[1], back_map[1])
    pair_map_out[...] = jnp.where(first, back_map[0], ahead_map[0])
    pair_off_out[...] = jnp.where(first, back_map[1], ahead_map[1]).astype(BF16)

    def to_side(index, source, target, device):
        return pltpu.make_async_remote_copy(
            src_ref=source,
            dst_ref=target,
            send_sem=side_send.at[index],
            recv_sem=side_recv.at[index],
            device_id=device,
            device_id_type=MESH,
        )

    pair_copies = [
        to_side(0, pair_map_out, pair_map_in, partner),
        to_side(1, pair_off_out, pair_off_in, partner),
    ]
    for copy in pair_copies:
        copy.start()
    for copy in pair_copies:
        copy.wait()
    through_map[...] = triple(pair_map_in[...], own_map)
    through_off[...] = triple(pair_map_in[...], own_off) + pair_off_in[...].astype(F32)
    until_map[...] = (
        lax.broadcasted_iota(jnp.int32, until_map.shape, 0)
        == lax.broadcasted_iota(jnp.int32, until_map.shape, 1)
    ).astype(F32)
    until_off[...] = jnp.zeros_like(until_off)

    levels = chips.bit_length() - 1

    def level_copy(kind, level, step):
        out, into = ((level_off_out, level_off_in), (level_map_out, level_map_in))[kind]
        return pltpu.make_async_remote_copy(
            src_ref=out.at[level],
            dst_ref=into.at[level],
            send_sem=level_send.at[kind, 2**level - 1 + step - 1],
            recv_sem=level_recv.at[kind, level],
            device_id={"outer": lax.rem(chip + toward * step + chips, chips) * 2 + core},
            device_id_type=MESH,
        )

    def extend_until(level):
        span = 2**level

        @pl.when(lax.rem(turn, 2 * span) >= span)
        def _():
            until_off[...] = until_off[...] + times(until_map[...], level_off_in[level])
            if level < levels - 1:
                @pl.when(turn >= 2 * span)
                def _():
                    until_map[...] = times(until_map[...], level_map_in[level])

    for level in range(levels):
        span = 2 ** level
        final = level == levels - 1
        place = lax.rem(turn, 2 * span)
        leading = turn < 2 * span

        @pl.when(place == span - 1)
        def _():
            level_off_out[level] = through_off[...].astype(BF16)
            if not final:
                level_map_out[level] = through_map[...].astype(BF16)
            for step in range(span, 0, -1):
                if not final:
                    @pl.when(jnp.logical_not(leading))
                    def _():
                        level_copy(1, level, step).start()
                level_copy(0, level, step).start()

        if level > 0:
            extend_until(level - 1)
        if final:
            share_map[...] = triple(own_map, until_map[...])
            share_off[...] = triple(own_map, until_off[...]) + own_off

        @pl.when(place >= span)
        def _():
            if not final:
                @pl.when(jnp.logical_not(leading))
                def _():
                    level_copy(1, level, 1).wait_recv()
            level_copy(0, level, 1).wait_recv()
            got = level_off_in[level]
            if final:
                share_off[...] = share_off[...] + times(share_map[...], got)
            else:
                @pl.when(place == 2 * span - 1)
                def _():
                    through_off[...] = through_off[...] + times(through_map[...], got)

                    @pl.when(jnp.logical_not(leading))
                    def _():
                        through_map[...] = times(through_map[...], level_map_in[level])

    share_out[...] = share_off[...].astype(BF16)
    swap = to_side(2, share_out, share_in, partner)
    swap.start()
    extend_until(levels - 1)
    swap.wait()
    carried = until_off[...]
    other = share_in[...].astype(F32)
    state = jnp.where(first, carried, other)
    end_grad = jnp.where(first, other, carried)
    d_query, d_key, d_value, d_decay, d_beta = delta_finish(kept, state, end_grad)

    for level in range(levels):
        span = 2 ** level

        @pl.when(lax.rem(turn, 2 * span) == span - 1)
        def _():
            for step in range(span, 0, -1):
                level_copy(0, level, step).wait_send()
                if level < levels - 1:
                    @pl.when(jnp.logical_not(turn < 2 * span))
                    def _():
                        level_copy(1, level, step).wait_send()

    grads = jnp.concatenate([d_query, d_key, d_value], axis=1).astype(BF16)
    d_decay = d_decay.astype(BF16).astype(F32)
    d_beta = d_beta.astype(BF16).astype(F32)

    def back_block(at):
        block = lax.dot_general(grads, main_w[at, :], NT, preferred_element_type=F32)
        return block + d_decay * gates_w[0:1, at] + d_beta * gates_w[1:2, at]

    hops = []
    for way in range(2):
        partial_half(way, back_block)
        hops.append(reduce_send(3, heap_two, way))
    back = reduce_finish(3, heap_two, last_two, hops)
    mixed = mixed_own[...]
    inv_two = lax.rsqrt(row_sum(mixed * mixed) * (1.0 / width) + EPS)
    gained = back * gain_two_ref[...]
    inner_sum = row_sum(mixed * gained) * (1.0 / width)
    grad_mixed[own_rows, :] = (
        inv_two * gained - mixed * (inv_two * inv_two * inv_two * inner_sum)
    ).astype(BF16)
    spread(4, row_piece(grad_mixed))
    out_ref[...] = hidden[...] * lax.dot_general(
        down_w[...], grad_mixed[...], NT, preferred_element_type=F32
    )


def shards(
    tokens, step_index, embed_table, gain_one, gate_weight, up_weight, down_weight, gain_two,
    query_weight, key_weight, value_weight, decay_weight, beta_weight, rate_log, decay_bias,
    beta_bias, cotangent,
):
    peers = lax.axis_size("inner")
    side = int(round(peers**0.5))
    chips = lax.axis_size("outer") // 2
    rows = tokens.shape[0]
    words, slab = embed_table.shape
    width = slab * peers
    hidden_dim = gate_weight.shape[1]
    key_dim, value_dim = query_weight.shape[1], value_weight.shape[1]
    share = rows // peers
    in_vmem = pl.BlockSpec(memory_space=pltpu.VMEM)
    in_smem = pl.BlockSpec(memory_space=pltpu.SMEM)
    in_place = pl.BlockSpec(memory_space=pl.ANY)
    vm = pltpu.VMEM
    messages = (side + 1) * (side - 1)
    levels = chips.bit_length() - 1
    state = (key_dim, value_dim)
    attribution = pl.pallas_call(
        functools.partial(kernel, chips),
        out_shape=jax.ShapeDtypeStruct((hidden_dim, rows), F32),
        in_specs=[in_place] + [in_smem] * 4 + [in_place] * 12,
        out_specs=in_vmem,
        scratch_shapes=[
            pltpu.SMEM((rows,), jnp.int32),
            vm((1, width), F32),
            vm((1, width), F32),
            vm((1, width), BF16),
            vm((1, width), BF16),
            vm((words // 8, 8, slab), BF16),
            vm((hidden_dim, width), BF16),
            vm((hidden_dim, width), BF16),
            vm((hidden_dim, width), BF16),
            vm((width, 2 * key_dim + value_dim), BF16),
            vm((rows, value_dim), BF16),
            vm((8, width), F32),
            vm((peers, rows, slab), BF16),
            vm((rows, width), BF16),
            vm((hidden_dim, rows), F32),
            vm((2, side, side, share, width // 2), BF16),
            vm((2, side * (side - 1), share, width // 2), BF16),
            vm((2, side * (side - 1), share, width // 2), BF16),
            vm((2, side - 1, share, width // 2), BF16),
            vm((2, side - 1, share, width // 2), BF16),
            vm((2, side - 1, share, width // 2), BF16),
            vm((rows, width), BF16),
            vm((rows, width), BF16),
            vm((share, width), F32),
            vm((key_dim, key_dim), F32),
            vm((key_dim, key_dim), F32),
            vm(state, BF16),
            vm(state, BF16),
            vm((key_dim, key_dim), F32),
            vm(state, F32),
            vm((key_dim, key_dim), F32),
            vm(state, F32),
            vm((key_dim, key_dim), F32),
            vm(state, F32),
            vm((levels, key_dim, key_dim), BF16),
            vm((levels, key_dim, key_dim), BF16),
            vm((levels,) + state, BF16),
            vm((levels,) + state, BF16),
            vm(state, BF16),
            vm(state, BF16),
            pltpu.SemaphoreType.DMA((5,)),
            pltpu.SemaphoreType.DMA((8,)),
            pltpu.SemaphoreType.DMA((5, 2, messages)),
            pltpu.SemaphoreType.DMA((5, 2, messages)),
            pltpu.SemaphoreType.DMA((3,)),
            pltpu.SemaphoreType.DMA((3,)),
            pltpu.SemaphoreType.DMA((2, chips - 1)),
            pltpu.SemaphoreType.DMA((2, levels)),
        ],
        compiler_params=pltpu.CompilerParams(collective_id=0, has_side_effects=True),
        name="attribution",
    )(
        tokens,
        step_index,
        rate_log,
        decay_bias,
        beta_bias,
        gain_one.reshape(1, width),
        gain_two.reshape(1, width),
        decay_weight.reshape(1, width),
        beta_weight.reshape(1, width),
        embed_table.reshape(words // 8, 8, slab),
        gate_weight.T,
        up_weight.T,
        down_weight,
        query_weight,
        key_weight,
        value_weight,
        cotangent,
    )
    return attribution.T


def solution(mesh):
    placed = (
        P("outer"), P(), P(None, "inner"), P(), P(None, "inner"), P(None, "inner"),
        P("inner", None), P(), P(None, "inner"), P(None, "inner"), P(None, "inner"),
        P(None, "inner"), P(None, "inner"), P("inner"), P("inner"), P("inner"),
        P("outer", "inner"),
    )
    return jax.shard_map(
        shards, mesh=mesh, in_specs=placed, out_specs=P("outer", "inner"), check_vma=False
    )
```

```python
import functools

import jax
import jax.numpy as jnp
from jax import lax
from jax.experimental import pallas as pl
from jax.experimental.pallas import tpu as pltpu
from jax.sharding import PartitionSpec as P

STEPS = 32
EPS = 1e-06
F32 = jnp.float32
BF16 = jnp.bfloat16
MESH = pl.DeviceIdType.MESH
HIGHEST = lax.Precision.HIGHEST
NN = (((1,), (0,)), ((), ()))
NT = (((1,), (1,)), ((), ()))
TN = (((0,), (0,)), ((), ()))


def exact(left, right, dims=NN):
    return lax.dot_general(left, right, dims, precision=HIGHEST, preferred_element_type=F32)


def fast(left, right, dims=NN):
    return lax.dot_general(
        left.astype(BF16), right.astype(BF16), dims, preferred_element_type=F32
    )


def row_sum(values):
    return jnp.sum(values, axis=1, keepdims=True)


def split(value):
    high = value.astype(BF16)
    return high, (value - high.astype(F32)).astype(BF16)


def triple(left, right, dims=NN):
    left_high, left_low = split(left)
    right_high, right_low = split(right)

    def dot(one, two):
        return lax.dot_general(one, two, dims, preferred_element_type=F32)

    return dot(left_high, right_high) + (dot(left_high, right_low) + dot(left_low, right_high))


def times(left, right):
    high, low = split(left)
    return jnp.dot(high, right, preferred_element_type=F32) + jnp.dot(
        low, right, preferred_element_type=F32
    )


def apply(left, right):
    high, low = split(right)
    return jnp.dot(left, high, preferred_element_type=F32) + jnp.dot(
        left, low, preferred_element_type=F32
    )


def running(ones, column):
    wide = jnp.broadcast_to(column, (column.shape[0], 128))
    high, rest = wide.astype(BF16), wide
    total = None
    for _ in range(3):
        high = rest.astype(BF16)
        rest = rest - high.astype(F32)
        term = jnp.dot(ones, high, preferred_element_type=F32)
        total = term if total is None else total + term
    return total


near = fast
solve = triple
gram = triple


def unit_inverse(lower):
    size = lower.shape[0]
    if size > 128:
        middle = size // 2
        upper_left = unit_inverse(lower[:middle, :middle])
        lower_right = unit_inverse(lower[middle:, middle:])
        below = -solve(lower_right, solve(lower[middle:, :middle], upper_left))
        top = jnp.concatenate([upper_left, jnp.zeros_like(below)], axis=1)
        return jnp.concatenate([top, jnp.concatenate([below, lower_right], axis=1)], axis=0)
    apart = lax.broadcasted_iota(jnp.int32, (size, size), 0) ^ lax.broadcasted_iota(
        jnp.int32, (size, size), 1
    )
    inverse = jnp.where(apart == 0, 1.0, 0.0) - jnp.where(apart == 1, lower, 0.0)
    for level in range(1, size.bit_length() - 1):
        joined = jnp.where(lax.shift_right_logical(apart, level) == 1, lower, 0.0)
        inverse = inverse - solve(inverse, solve(joined, inverse))
    return inverse


def delta_prepare(query_pre, key_pre, values, decay_pre, beta_pre, cot, rate, decay_bias, beta_bias):
    size, key_dim = key_pre.shape
    query_inv = lax.rsqrt(row_sum(query_pre * query_pre) + EPS)
    key_inv = lax.rsqrt(row_sum(key_pre * key_pre) + EPS)
    queries = query_pre * (query_inv * key_dim ** (-0.5))
    keys = key_pre * key_inv
    shifted = decay_pre + decay_bias
    soft = jnp.maximum(shifted, 0.0) + jnp.log1p(jnp.exp(-jnp.abs(shifted)))
    log_decay = -jnp.exp(rate) * soft
    betas = 1.0 / (1.0 + jnp.exp(-(beta_pre + beta_bias)))

    rows = lax.broadcasted_iota(jnp.int32, (size, size), 0)
    cols = lax.broadcasted_iota(jnp.int32, (size, size), 1)
    lower = rows >= cols
    cum_wide = running(lower.astype(F32).astype(BF16), log_decay)
    cum_rows = jnp.concatenate([cum_wide] * (size // 128), axis=1)
    cum_cols = jnp.concatenate([cum_wide.T] * (size // 128), axis=0)
    ratio = jnp.where(lower, jnp.exp(jnp.where(lower, cum_rows - cum_cols, 0.0)), 0.0)
    cum = cum_rows[:, 0:1]
    cum_last = cum_cols[:, size - 1 : size]
    grown = jnp.exp(cum)
    left_over = jnp.exp(cum_last - cum)
    total = jnp.exp(cum_last[0:1, :])

    key_gram = gram(keys, keys, NT)
    ratio_gram = jnp.where(rows > cols, ratio * key_gram, 0.0)
    strict = betas * ratio_gram
    inverse = unit_inverse(strict)
    scores = ratio * near(queries, keys, NT)
    keys_grown = grown * keys
    queries_grown = grown * queries
    keys_tail = left_over * keys

    fresh_free = solve(inverse, betas * values)
    fresh_map = solve(inverse, betas * keys_grown)
    back_free = solve(inverse, near(scores, cot, TN), TN)
    back_map = solve(inverse, keys_tail, TN)
    eye = (
        lax.broadcasted_iota(jnp.int32, (key_dim, key_dim), 0)
        == lax.broadcasted_iota(jnp.int32, (key_dim, key_dim), 1)
    ).astype(F32)
    transition = total * eye - near(keys_tail, fresh_map, TN)
    transition_back = total * eye - near(fresh_map, keys_tail, TN)
    offset = near(keys_tail, fresh_free, TN)
    offset_back = near(queries_grown, cot, TN) - near(betas * keys_grown, back_free, TN)
    kept = dict(
        query_pre=query_pre, key_pre=key_pre, values=values, query_inv=query_inv, key_inv=key_inv,
        queries=queries, keys=keys, shifted=shifted, betas=betas, ratio=ratio, grown=grown,
        left_over=left_over, total=total, ratio_gram=ratio_gram, strict=strict, scores=scores,
        keys_grown=keys_grown, keys_tail=keys_tail, fresh_free=fresh_free, fresh_map=fresh_map,
        back_free=back_free, back_map=back_map, cot=cot, rate=rate,
    )
    return kept, (transition, offset), (transition_back, offset_back)


def delta_finish(kept, state, end_grad):
    k = kept
    size, key_dim = k["keys"].shape
    scale = key_dim ** (-0.5)
    rows = lax.broadcasted_iota(jnp.int32, (size, size), 0)
    cols = lax.broadcasted_iota(jnp.int32, (size, size), 1)
    fresh = k["fresh_free"] - near(k["fresh_map"], state)
    back = k["back_free"] + near(k["back_map"], end_grad)
    d_strict = jnp.where(rows > cols, -near(back, fresh, NT), 0.0)
    d_gram = d_strict * (k["betas"] * k["ratio"])
    d_scores = near(k["cot"], fresh, NT) * k["ratio"]
    residual = k["values"] - near(k["keys_grown"], state)
    d_values = k["betas"] * back
    d_betas = row_sum(back * residual) + row_sum(d_strict * k["ratio_gram"])
    cot_state = k["grown"] * near(k["cot"], state, NT)
    back_state = (k["grown"] * k["betas"]) * near(back, state, NT)
    fresh_end = k["left_over"] * near(fresh, end_grad, NT)
    d_queries = near(d_scores, k["keys"]) + cot_state
    d_keys_read = near(d_gram, k["keys"]) - back_state
    d_keys_write = near(d_gram, k["keys"], TN) + near(d_scores, k["queries"], TN) + fresh_end
    d_cum = row_sum(k["queries"] * d_queries) + row_sum(k["keys"] * (d_keys_read - d_keys_write))
    ends = jnp.sum(row_sum(k["keys"] * fresh_end), axis=0, keepdims=True) + k["total"] * jnp.sum(
        row_sum(state * end_grad), axis=0, keepdims=True
    )
    upper = (rows <= cols).astype(F32).astype(BF16)
    d_log = running(upper, d_cum)[:, 0:1] + ends

    query_inv, key_inv = k["query_inv"], k["key_inv"]
    d_query = (scale * query_inv) * (
        d_queries - k["query_pre"] * (query_inv * query_inv * row_sum(k["query_pre"] * d_queries))
    )
    d_keys = d_keys_read + d_keys_write
    d_key = key_inv * (d_keys - k["keys"] * row_sum(k["keys"] * d_keys))
    d_decay = d_log * (-jnp.exp(k["rate"])) * (1.0 / (1.0 + jnp.exp(-k["shifted"])))
    d_beta = d_betas * k["betas"] * (1.0 - k["betas"])
    return d_query, d_key, d_values, d_decay, d_beta


def ring_order(side):
    return sorted(range(1, side), key=lambda step: (-min(step, side - step), step))


def kernel(
    chips,
    tokens_hbm, step_ref, rate_ref, decay_bias_ref, beta_bias_ref, gain_one_hbm, gain_two_hbm,
    decay_hbm, beta_hbm, table_hbm, gate_hbm, up_hbm, down_hbm, query_hbm, key_hbm, value_hbm,
    cot_hbm,
    out_ref,
    tokens_ref, gain_one_ref, gain_two_ref, decay_ref, beta_ref, table, gate_w, up_w, down_w, main_w, cot_v, gates_w, emb, normed, hidden, part,
    heap_one, heap_two, sums, last_one, last_two,
    normed_two, grad_mixed, mixed_own, pair_map_out, pair_map_in, pair_off_out,
    pair_off_in, until_map, until_off, share_map, share_off, through_map, through_off, map_out, map_in,
    off_out, off_in, middle_out, middle_in, share_out, share_in,
    small_sem, load_sem, send_sem, recv_sem, side_send, side_recv, group_send, group_recv,
    middle_send, middle_recv,
):
    me = lax.axis_index("inner")
    outer = lax.axis_index("outer")
    peers = lax.axis_size("inner")
    side = int(round(peers**0.5))
    line, spot = me // side, lax.rem(me, side)
    chip, core = outer // 2, lax.rem(outer, 2)
    partner = {"outer": outer + 1 - 2 * core}
    turn = chip + core * (chips - 1 - 2 * chip)
    toward = 1 - 2 * core

    key_dim = query_hbm.shape[1]
    value_dim = value_hbm.shape[1]
    width = down_hbm.shape[1]
    half = width // 2
    rows = tokens_ref.shape[0]
    share = rows // peers
    slab = table.shape[2]

    barrier = pltpu.get_barrier_semaphore()
    for step in range(1, side):
        for peer in (
            lax.rem(line + step, side) * side + spot,
            line * side + lax.rem(spot + step, side),
        ):
            pl.semaphore_signal(barrier, inc=1, device_id={"inner": peer}, device_id_type=MESH)
    pl.semaphore_signal(barrier, inc=1, device_id=partner, device_id_type=MESH)
    for step in range(1, chips):
        device = {"outer": lax.rem(chip + step, chips) * 2 + core}
        pl.semaphore_signal(barrier, inc=1, device_id=device, device_id_type=MESH)

    small = [
        pltpu.make_async_copy(source, target, small_sem.at[index])
        for index, (source, target) in enumerate((
            (tokens_hbm, tokens_ref), (gain_one_hbm, gain_one_ref), (gain_two_hbm, gain_two_ref),
            (decay_hbm, decay_ref), (beta_hbm, beta_ref),
        ))
    ]
    small[0].start()
    loads = [
        pltpu.make_async_copy(gate_hbm, gate_w, load_sem.at[0]),
        pltpu.make_async_copy(up_hbm, up_w, load_sem.at[1]),
        pltpu.make_async_copy(down_hbm, down_w, load_sem.at[2]),
        pltpu.make_async_copy(query_hbm, main_w.at[:, pl.ds(0, key_dim)], load_sem.at[3]),
        pltpu.make_async_copy(key_hbm, main_w.at[:, pl.ds(key_dim, key_dim)], load_sem.at[4]),
        pltpu.make_async_copy(value_hbm, main_w.at[:, pl.ds(2 * key_dim, value_dim)], load_sem.at[5]),
        pltpu.make_async_copy(cot_hbm, cot_v, load_sem.at[6]),
    ]
    table_load = pltpu.make_async_copy(table_hbm, table, load_sem.at[7])
    table_load.start()
    for load in small[1:]:
        load.start()
    for load in loads:
        load.start()

    for load in small:
        load.wait()
    row_id = lax.broadcasted_iota(jnp.int32, (8, width), 0)
    gates_w[...] = jnp.where(
        row_id == 0,
        decay_ref[...].astype(F32),
        jnp.where(row_id == 1, beta_ref[...].astype(F32), 0.0),
    )

    table_load.wait()
    tile_row = lax.broadcasted_iota(jnp.int32, (8, slab), 0)

    def pick(index, carry):
        found = []
        for part_of in range(2):
            tile = jnp.zeros((8, slab), F32)
            for row in range(8):
                token = tokens_ref[index * 16 + part_of * 8 + row]
                near_rows = table[lax.shift_right_logical(token, 3)].astype(F32)
                chosen = jnp.sum(
                    jnp.where(tile_row == (token & 7), near_rows, 0.0), axis=0, keepdims=True
                )
                tile = jnp.where(tile_row == row, chosen, tile)
            found.append(tile)
        emb[me, pl.ds(pl.multiple_of(index * 16, 16), 16), :] = jnp.concatenate(
            found, axis=0
        ).astype(BF16)
        return carry

    lax.fori_loop(0, rows // 16, pick, 0)
    pl.semaphore_wait(barrier, 2 * (side - 1) + chips)

    def to_axis(across, step):
        if across:
            return line * side + lax.rem(spot + step, side)
        return lax.rem(line + step, side) * side + spot

    def send(stage, way, index, source, target, peer):
        copy = pltpu.make_async_remote_copy(
            src_ref=source,
            dst_ref=target,
            send_sem=send_sem.at[stage, way, index],
            recv_sem=recv_sem.at[stage, way, index],
            device_id={"inner": peer},
            device_id_type=MESH,
        )
        copy.start()
        return copy

    order = ring_order(side)

    def spread(stage, piece):
        first_hop, second_hop = [{}, {}], []
        for step in order:
            for way in range(2):
                own = piece(me, way)
                first_hop[way][step] = send(stage, way, step - 1, own, own, to_axis(way, step))
        for step in order:
            for way in range(2):
                own = piece(me, way)
                second_hop.append(
                    send(stage, way, side - 1 + step - 1, own, own, to_axis(1 - way, step))
                )
        for gone in reversed(order):
            for way in range(2):
                first_hop[way][gone].wait_recv()
                got = piece(to_axis(way, side - gone), way)
                for step in order:
                    index = (side - 1) * (1 + gone) + step - 1
                    second_hop.append(send(stage, way, index, got, got, to_axis(1 - way, step)))
        for copy in second_hop:
            copy.wait()
        for way in range(2):
            for step in order:
                first_hop[way][step].wait_send()

    def reduce_send(stage, heap, way):
        hops = {}
        for apart in order + [0]:
            for step in order:
                if way == 0:
                    at = (lax.rem(line + apart, side), lax.rem(spot + step, side))
                else:
                    at = (lax.rem(line + step, side), lax.rem(spot + apart, side))
                index = apart * (side - 1) + step - 1
                hops[apart, step] = send(
                    stage, way, index, part.at[way, at[0], at[1]], heap.at[way, index],
                    to_axis(1 - way, step),
                )
        return hops

    def reduce_finish(stage, heap, last, hops):
        own, second_hop = [None, None], [[], []]
        for apart in order + [0]:
            for way in range(2):
                if way == 0:
                    at = (lax.rem(line + apart, side), spot)
                else:
                    at = (line, lax.rem(spot + apart, side))
                total = part[way, at[0], at[1]].astype(F32)
                for step in reversed(order):
                    hops[way][apart, step].wait_recv()
                    total = total + heap[way, apart * (side - 1) + step - 1].astype(F32)
                if apart == 0:
                    own[way] = total
                else:
                    sums[way, apart - 1] = total.astype(BF16)
                    second_hop[way].append(
                        (apart, send(
                            stage, way, side * (side - 1) + apart - 1, sums.at[way, apart - 1],
                            last.at[way, apart - 1], to_axis(way, apart),
                        ))
                    )
        for way in range(2):
            for apart, copy in second_hop[way]:
                copy.wait()
                own[way] = own[way] + last[way, apart - 1].astype(F32)
            for copy in hops[way].values():
                copy.wait_send()
        return jnp.concatenate(own, axis=1)

    spread(0, lambda owner, way: emb.at[owner, pl.ds(way * (rows // 2), rows // 2), :])

    def norm_one(index, carry):
        at = pl.ds(pl.multiple_of(index * 16, 16), 16)
        values = [emb[owner, at, :].astype(F32) for owner in range(peers)]
        squares = values[0] * values[0]
        for value in values[1:]:
            squares = squares + value * value
        scale = lax.rsqrt(row_sum(squares) * (1.0 / width) + EPS)
        for owner, value in enumerate(values):
            cut = slice(owner * slab, (owner + 1) * slab)
            normed[at, cut] = (value * scale * gain_one_ref[:, cut]).astype(BF16)
        return carry

    lax.fori_loop(0, rows // 16, norm_one, 0, unroll=2)
    loads[0].wait()
    loads[1].wait()
    gate_rows = lax.dot_general(normed[...], gate_w[...], NT, preferred_element_type=F32)
    up_rows = lax.dot_general(normed[...], up_w[...], NT, preferred_element_type=F32)
    active = gate_rows * (1.0 / (1.0 + jnp.exp(-gate_rows))) * up_rows
    path_scale = (step_ref[0].astype(F32) + 0.5) / STEPS
    scaled = (path_scale * active).astype(BF16)
    loads[2].wait()

    def partial_half(way, product):
        for first in range(way * half, way * half + half, 256):
            block = product(slice(first, first + 256)).astype(BF16)
            at = slice(first - way * half, first - way * half + 256)
            part[way, :, :, :, at] = block.reshape(side, side, share, 256)

    hops = []
    for way in range(2):
        partial_half(
            way, lambda at: jnp.dot(scaled, down_w[:, at], preferred_element_type=F32)
        )
        hops.append(reduce_send(1, heap_one, way))
    hidden[...] = active.T
    own_rows = pl.ds(pl.multiple_of(me * share, share), share)
    own_emb = jnp.concatenate([emb[owner, own_rows, :] for owner in range(peers)], axis=1)
    mixed = own_emb.astype(F32) + reduce_finish(1, heap_one, last_one, hops)
    mixed_own[...] = mixed
    inv_two = lax.rsqrt(row_sum(mixed * mixed) * (1.0 / width) + EPS)
    normed_two[own_rows, :] = (mixed * inv_two * gain_two_ref[...]).astype(BF16)

    def row_piece(array):
        return lambda owner, way: array.at[
            pl.ds(pl.multiple_of(owner * share, share), share), pl.ds(way * half, half)
        ]

    spread(2, row_piece(normed_two))
    for load in loads[3:]:
        load.wait()
    main = jnp.dot(normed_two[...], main_w[...], preferred_element_type=F32)
    gates = lax.dot_general(
        normed_two[...], gates_w[...].astype(BF16), NT, preferred_element_type=F32
    )
    kept, ahead_map, back_map = delta_prepare(
        main[:, :key_dim],
        main[:, key_dim : 2 * key_dim],
        main[:, 2 * key_dim :],
        gates[:, 0:1],
        gates[:, 1:2],
        cot_v[...].astype(F32),
        jnp.full((1, 1), rate_ref[0]),
        decay_bias_ref[0],
        beta_bias_ref[0],
    )

    first = core == 0
    own_map = jnp.where(first, ahead_map[0], back_map[0])
    own_off = jnp.where(first, ahead_map[1], back_map[1])
    pair_map_out[...] = jnp.where(first, back_map[0], ahead_map[0])
    pair_off_out[...] = jnp.where(first, back_map[1], ahead_map[1]).astype(BF16)

    def to_side(index, source, target, device):
        return pltpu.make_async_remote_copy(
            src_ref=source,
            dst_ref=target,
            send_sem=side_send.at[index],
            recv_sem=side_recv.at[index],
            device_id=device,
            device_id_type=MESH,
        )

    pair_copies = [
        to_side(0, pair_map_out, pair_map_in, partner),
        to_side(1, pair_off_out, pair_off_in, partner),
    ]
    for copy in pair_copies:
        copy.start()
    for copy in pair_copies:
        copy.wait()
    through_map[...] = triple(pair_map_in[...], own_map)
    through_off[...] = triple(pair_map_in[...], own_off) + pair_off_in[...].astype(F32)
    until_map[...] = (
        lax.broadcasted_iota(jnp.int32, until_map.shape, 0)
        == lax.broadcasted_iota(jnp.int32, until_map.shape, 1)
    ).astype(F32)
    until_off[...] = jnp.zeros_like(until_off)

    group = chips // 2
    place = lax.rem(turn, group)
    early = turn < group
    map_out[...] = through_map[...].astype(BF16)
    off_out[...] = through_off[...].astype(BF16)

    def along(step):
        return {"outer": lax.rem(chip + toward * step + chips, chips) * 2 + core}

    def group_copy(kind, apart):
        out, into = ((off_out, off_in), (map_out, map_in))[kind]
        return pltpu.make_async_remote_copy(
            src_ref=out,
            dst_ref=into.at[apart - 1],
            send_sem=group_send.at[kind, apart - 1],
            recv_sem=group_recv.at[kind, apart - 1],
            device_id=along(apart),
            device_id_type=MESH,
        )

    def middle_copy(step):
        return pltpu.make_async_remote_copy(
            src_ref=middle_out,
            dst_ref=middle_in,
            send_sem=middle_send.at[step - 1],
            recv_sem=middle_recv.at[0],
            device_id=along(step),
            device_id_type=MESH,
        )

    for apart in range(group - 1, 0, -1):
        @pl.when(place + apart < group)
        def _():
            @pl.when(turn > 0)
            def _():
                group_copy(1, apart).start()
            group_copy(0, apart).start()

    for apart in range(group - 1, 0, -1):
        @pl.when(place >= apart)
        def _():
            @pl.when(turn > apart)
            def _():
                group_copy(1, apart).wait_recv()
            group_copy(0, apart).wait_recv()

            @pl.when(place == apart)
            def _():
                until_off[...] = off_in[apart - 1].astype(F32)

                @pl.when(jnp.logical_not(early))
                def _():
                    until_map[...] = map_in[apart - 1].astype(F32)

            @pl.when(place > apart)
            def _():
                got_map = map_in[apart - 1]
                until_off[...] = apply(got_map, until_off[...]) + off_in[apart - 1].astype(F32)

                @pl.when(jnp.logical_not(early))
                def _():
                    until_map[...] = apply(got_map, until_map[...])

    @pl.when(turn == group - 1)
    def _():
        middle_out[...] = (triple(through_map[...], until_off[...]) + through_off[...]).astype(BF16)
        for step in range(group, 0, -1):
            middle_copy(step).start()

    share_map[...] = triple(own_map, until_map[...])
    share_off[...] = triple(own_map, until_off[...]) + own_off

    @pl.when(turn >= group)
    def _():
        middle_copy(1).wait_recv()
        share_off[...] = share_off[...] + times(share_map[...], middle_in[...])

    share_out[...] = share_off[...].astype(BF16)
    swap = to_side(2, share_out, share_in, partner)
    swap.start()

    @pl.when(turn >= group)
    def _():
        until_off[...] = until_off[...] + times(until_map[...], middle_in[...])

    swap.wait()
    carried = until_off[...]
    other = share_in[...].astype(F32)
    state = jnp.where(first, carried, other)
    end_grad = jnp.where(first, other, carried)
    d_query, d_key, d_value, d_decay, d_beta = delta_finish(kept, state, end_grad)

    for apart in range(group - 1, 0, -1):
        @pl.when(place + apart < group)
        def _():
            @pl.when(turn > 0)
            def _():
                group_copy(1, apart).wait_send()
            group_copy(0, apart).wait_send()

    @pl.when(turn == group - 1)
    def _():
        for step in range(group, 0, -1):
            middle_copy(step).wait_send()

    grads = jnp.concatenate([d_query, d_key, d_value], axis=1).astype(BF16)
    d_decay = d_decay.astype(BF16).astype(F32)
    d_beta = d_beta.astype(BF16).astype(F32)

    def back_block(at):
        block = lax.dot_general(grads, main_w[at, :], NT, preferred_element_type=F32)
        return block + d_decay * gates_w[0:1, at] + d_beta * gates_w[1:2, at]

    hops = []
    for way in range(2):
        partial_half(way, back_block)
        hops.append(reduce_send(3, heap_two, way))
    back = reduce_finish(3, heap_two, last_two, hops)
    mixed = mixed_own[...]
    inv_two = lax.rsqrt(row_sum(mixed * mixed) * (1.0 / width) + EPS)
    gained = back * gain_two_ref[...]
    inner_sum = row_sum(mixed * gained) * (1.0 / width)
    grad_mixed[own_rows, :] = (
        inv_two * gained - mixed * (inv_two * inv_two * inv_two * inner_sum)
    ).astype(BF16)
    spread(4, row_piece(grad_mixed))
    out_ref[...] = hidden[...] * lax.dot_general(
        down_w[...], grad_mixed[...], NT, preferred_element_type=F32
    )


def shards(
    tokens, step_index, embed_table, gain_one, gate_weight, up_weight, down_weight, gain_two,
    query_weight, key_weight, value_weight, decay_weight, beta_weight, rate_log, decay_bias,
    beta_bias, cotangent,
):
    peers = lax.axis_size("inner")
    side = int(round(peers**0.5))
    chips = lax.axis_size("outer") // 2
    rows = tokens.shape[0]
    words, slab = embed_table.shape
    width = slab * peers
    hidden_dim = gate_weight.shape[1]
    key_dim, value_dim = query_weight.shape[1], value_weight.shape[1]
    share = rows // peers
    in_vmem = pl.BlockSpec(memory_space=pltpu.VMEM)
    in_smem = pl.BlockSpec(memory_space=pltpu.SMEM)
    in_place = pl.BlockSpec(memory_space=pl.ANY)
    vm = pltpu.VMEM
    messages = (side + 1) * (side - 1)
    group = chips // 2
    state = (key_dim, value_dim)
    attribution = pl.pallas_call(
        functools.partial(kernel, chips),
        out_shape=jax.ShapeDtypeStruct((hidden_dim, rows), F32),
        in_specs=[in_place] + [in_smem] * 4 + [in_place] * 12,
        out_specs=in_vmem,
        scratch_shapes=[
            pltpu.SMEM((rows,), jnp.int32),
            vm((1, width), F32),
            vm((1, width), F32),
            vm((1, width), BF16),
            vm((1, width), BF16),
            vm((words // 8, 8, slab), BF16),
            vm((hidden_dim, width), BF16),
            vm((hidden_dim, width), BF16),
            vm((hidden_dim, width), BF16),
            vm((width, 2 * key_dim + value_dim), BF16),
            vm((rows, value_dim), BF16),
            vm((8, width), F32),
            vm((peers, rows, slab), BF16),
            vm((rows, width), BF16),
            vm((hidden_dim, rows), F32),
            vm((2, side, side, share, width // 2), BF16),
            vm((2, side * (side - 1), share, width // 2), BF16),
            vm((2, side * (side - 1), share, width // 2), BF16),
            vm((2, side - 1, share, width // 2), BF16),
            vm((2, side - 1, share, width // 2), BF16),
            vm((2, side - 1, share, width // 2), BF16),
            vm((rows, width), BF16),
            vm((rows, width), BF16),
            vm((share, width), F32),
            vm((key_dim, key_dim), F32),
            vm((key_dim, key_dim), F32),
            vm(state, BF16),
            vm(state, BF16),
            vm((key_dim, key_dim), F32),
            vm(state, F32),
            vm((key_dim, key_dim), F32),
            vm(state, F32),
            vm((key_dim, key_dim), F32),
            vm(state, F32),
            vm((key_dim, key_dim), BF16),
            vm((group - 1, key_dim, key_dim), BF16),
            vm(state, BF16),
            vm((group - 1,) + state, BF16),
            vm(state, BF16),
            vm(state, BF16),
            vm(state, BF16),
            vm(state, BF16),
            pltpu.SemaphoreType.DMA((5,)),
            pltpu.SemaphoreType.DMA((8,)),
            pltpu.SemaphoreType.DMA((5, 2, messages)),
            pltpu.SemaphoreType.DMA((5, 2, messages)),
            pltpu.SemaphoreType.DMA((3,)),
            pltpu.SemaphoreType.DMA((3,)),
            pltpu.SemaphoreType.DMA((2, group - 1)),
            pltpu.SemaphoreType.DMA((2, group - 1)),
            pltpu.SemaphoreType.DMA((group,)),
            pltpu.SemaphoreType.DMA((1,)),
        ],
        compiler_params=pltpu.CompilerParams(collective_id=0, has_side_effects=True),
        name="attribution",
    )(
        tokens,
        step_index,
        rate_log,
        decay_bias,
        beta_bias,
        gain_one.reshape(1, width),
        gain_two.reshape(1, width),
        decay_weight.reshape(1, width),
        beta_weight.reshape(1, width),
        embed_table.reshape(words // 8, 8, slab),
        gate_weight.T,
        up_weight.T,
        down_weight,
        query_weight,
        key_weight,
        value_weight,
        cotangent,
    )
    return attribution.T


def solution(mesh):
    placed = (
        P("outer"), P(), P(None, "inner"), P(), P(None, "inner"), P(None, "inner"),
        P("inner", None), P(), P(None, "inner"), P(None, "inner"), P(None, "inner"),
        P(None, "inner"), P(None, "inner"), P("inner"), P("inner"), P("inner"),
        P("outer", "inner"),
    )
    return jax.shard_map(
        shards, mesh=mesh, in_specs=placed, out_specs=P("outer", "inner"), check_vma=False
    )
```
